128 devices in a mesh: grp: 16 (over z, x), reg: 8 (over y, core).
Axes of the slice: x: 4, y: 4, z: 4, core: 2. Of those that a mesh axis runs over, the one named last changes fastest.
Arguments:
- orbitals: bfloat16 [8, 16, 512, 1024], P('reg', 'grp'), may hold values from -6 to 6
- occupied: bfloat16 [8, 16, 8, 512], P('reg', 'grp'), may hold values from -0.59765625 to 0.59765625
- panel_index: int32 [128], replicated, may hold values from 0 to 1023, as said below
- screening: bfloat16 [896, 512, 512], P(('grp', 'reg')), may hold values from -0.25 to 0.25
- block_region: int32 [896, 1], P(('grp', 'reg')), may hold values from 0 to 7; in each aligned block of 7 rows (0 to 6, 7 to 13, ...) at most 2 rows name the same one
- block_row: int32 [896], P(('grp', 'reg')), may hold values from 0 to 15
- block_col: int32 [896], P(('grp', 'reg')), may hold values from 0 to 15
Outputs:
- sigma: float32 [8, 128, 128], P('reg')
The draws below stay inside these ranges and needn't reach their ends.
Inputs may be any that keep to these rules, and one draw needn't show every extreme that they name: `panel_index`: the 128 indices are distinct. Among the 7 blocks of one device (aligned rows of block_region), at most 2 name the same region.
All inputs are finite; a program needn't handle non-finite values.
Results may differ from the reference program's by a relative error of at most 0.0054.
Values may be sent and summed in bfloat16 or wider, within the bound.
A program may use at most 192 MiB of HBM per device.

```python
import math
import jax
import jax.numpy as jnp
import numpy as np
from jax import lax

PTS = 512
PANEL = 128
ORBS = 1024
OCC = 8
CAP = 2
NW_DEV = 7
REGIONS = 8
GRID_REG = 16
BLOCKS = 896


def draw_panel_index(key, part):
    stride = ORBS // PANEL
    offsets = jax.random.randint(key, (PANEL,), 0, stride)
    position = jnp.arange(PANEL)
    offsets = jnp.where(position == 0, 0, jnp.where(position == PANEL - 1, stride - 1, offsets))
    values = position * stride + offsets
    ranking = jax.random.permutation(jax.random.fold_in(key, 7), PANEL)
    return values[ranking].astype(jnp.int32)


def with_ends(array, rng, least, largest):
    extent = array.shape
    place = [jax.random.randint(jax.random.fold_in(rng, axis), (), 0, extent[axis]) for axis in range(len(extent))]
    array = array.at[tuple(place)].set(least)
    longest = extent.index(max(extent))
    place[longest] = (place[longest] + 1) % extent[longest]
    return array.at[tuple(place)].set(largest)


def level_of(rng, dims, split, low, top_value):
    def one(dim, shards_of):
        steps = jax.random.uniform(jax.random.fold_in(jax.random.fold_in(rng, 6), dim), (shards_of,), jnp.float32, low / len(split), top_value / len(split))
        return jnp.repeat(jnp.exp(steps), dims[dim] // shards_of).reshape((-1,) + (1,) * (len(dims) - dim - 1))

    gain = one(*split[0])
    for cut in split[1:]:
        gain = gain * one(*cut)
    return gain


def assign_block(rng, own, number, rows, number_of, top, limit, lean):
    order = jax.random.permutation(rng, number_of)
    crowded, common = portions_of(number_of, rows * top, limit, lean, True), portions_of(number_of, rows * top, limit, lean, False)
    places = jnp.arange(number_of)

    def named(tallies, offset_by):
        used = int((tallies > 0).sum())
        fixed = max(1, used // 4)
        passed = fixed + (places - fixed + offset_by * (used - fixed)) % max(1, number_of - fixed)
        return jnp.zeros((number_of,), jnp.int32).at[order[jnp.where(places < fixed, places, passed)]].set(jnp.asarray(tallies, jnp.int32))

    tallies = jnp.where(number % 4 == 0, named(crowded, number // 4), named(common, number - number // 4 - 1))
    mixed = jax.random.permutation(jax.random.fold_in(own, 3), number_of)
    giver, receiver = mixed[0:number_of // 2 * 2:2], mixed[1:number_of // 2 * 2:2]
    slack = jnp.minimum(tallies[giver] - 1, limit - tallies[receiver]) // 2
    slack = jnp.where((giver == order[0]) | (receiver == order[0]) | (tallies[receiver] == 0), 0, jnp.maximum(slack, 0))
    passed = jax.random.randint(jax.random.fold_in(own, 4), (number_of // 2,), 0, 1 << 20) % (slack + 1)
    tallies = tallies.at[giver].add(-passed).at[receiver].add(passed)
    items = jnp.searchsorted(jnp.cumsum(tallies), jnp.arange(rows * top), side="right").astype(jnp.int32)
    grid = items.reshape(top, rows).T
    grid = grid[jax.random.permutation(jax.random.fold_in(own, 1), rows)]
    offset_by = jax.random.randint(jax.random.fold_in(own, 2), (rows, 1), 0, top)
    return jnp.take_along_axis(grid, (jnp.arange(top)[None, :] + offset_by) % top, axis=1)


def portions_of(number_of, total, most, lean, full):
    loads = [(1 << 20) // math.isqrt(rank ** lean) + 1 for rank in range(1, number_of + 1)]
    largest = most if full else min(most, max(-(-total // number_of), total * loads[0] // sum(loads)))
    least = 1 if total - largest >= number_of - 1 else 0
    given, spare = [largest] + [least] * (number_of - 1), total - largest - least * (number_of - 1)
    while spare > 0:
        candidates = [i for i in range(1, number_of) if given[i] < largest] or [i for i in range(1, number_of) if given[i] < most]
        mass, left = sum([loads[i] for i in candidates]), spare
        for i in candidates:
            extra = min(most - given[i], max(1, left * loads[i] // mass), spare)
            given[i] = given[i] + extra
            spare = spare - extra
    return np.array(given)


def centred(rng, shape, spread, most, cuts=(), held_as=jnp.bfloat16):
    result = spread * jax.random.normal(rng, shape, jnp.float32)
    if cuts:
        result = result * level_of(rng, shape, cuts, -0.22, 0.18)
    return jnp.clip(result, -most, most).astype(held_as)


def setup_inputs(seed: int = 0) -> dict:
    streams_of = jax.random.split(jax.random.key(seed), 8)
    orbitals = centred(streams_of[0], (REGIONS, GRID_REG, PTS, ORBS), 1.0, 6.0, ((0, 8), (1, 16)))
    occupied = centred(streams_of[1], (REGIONS, GRID_REG, OCC, PTS), 0.1, 0.59765625, ((0, 8), (1, 16)))
    panel_index = draw_panel_index(jax.random.fold_in(streams_of[7], 71), 0)
    screening = centred(streams_of[3], (BLOCKS, PTS, PTS), PTS ** -0.5, 0.25, ((0, 128),))
    block_region_keys = jax.random.split(jax.random.fold_in(streams_of[4], 1), BLOCKS // NW_DEV)
    block_region_turns = jax.random.permutation(jax.random.fold_in(streams_of[4], 3), BLOCKS // NW_DEV)
    block_region = jax.vmap(lambda own, number: assign_block(jax.random.fold_in(streams_of[4], 2), own, number, NW_DEV, REGIONS, 1, CAP, 2))(block_region_keys, block_region_turns).reshape((BLOCKS, 1))
    block_row = with_ends(jax.random.randint(streams_of[5], (BLOCKS,), 0, GRID_REG), jax.random.fold_in(streams_of[5], 1), 0, GRID_REG - 1).astype(jnp.int32)
    block_col = with_ends(jax.random.randint(streams_of[6], (BLOCKS,), 0, GRID_REG), jax.random.fold_in(streams_of[6], 1), 0, GRID_REG - 1).astype(jnp.int32)
    return {"orbitals": orbitals, "occupied": occupied, "panel_index": panel_index, "screening": screening, "block_region": block_region, "block_row": block_row, "block_col": block_col}


def reference(orbitals, occupied, panel_index, screening, block_region, block_row, block_col):
    panel_orbs = jnp.take(orbitals, panel_index.astype(jnp.int32), axis=3)
    densities = (panel_orbs[:, :, :, None, :].astype(jnp.float32)
                 * jnp.swapaxes(occupied, 2, 3)[..., None].astype(jnp.float32)).astype(jnp.bfloat16)

    def accumulate(sigma, item):
        screen_tile, region, row_block, col_block = item
        col_pairs = densities[region, col_block].reshape(PTS, OCC * PANEL)
        screened = jnp.dot(screen_tile, col_pairs, preferred_element_type=jnp.float32).astype(jnp.bfloat16)
        row_pairs = densities[region, row_block].reshape(PTS * OCC, PANEL)
        contrib = jnp.dot(row_pairs.T, screened.reshape(PTS * OCC, PANEL), preferred_element_type=jnp.float32)
        return sigma.at[region].add(contrib), jnp.zeros((), jnp.float32)

    start_sigma = jnp.zeros((REGIONS, PANEL, PANEL), jnp.float32)
    sigma, unused = lax.scan(accumulate, start_sigma,
                             (screening, block_region[:, 0].astype(jnp.int32),
                              block_row.astype(jnp.int32), block_col.astype(jnp.int32)))
    return sigma
```

```python
import functools

import jax
import jax.numpy as jnp
from jax import lax
from jax.experimental import pallas as pl
from jax.experimental.pallas import tpu as pltpu
from jax.sharding import PartitionSpec as P

MESH = pl.DeviceIdType.MESH
SIDE = 4
ORDERS = (("x", "y", "z"), ("y", "z", "x"), ("z", "x", "y"))
STEPS = (1, -1, 2)


def mod4(v):
    return lax.rem(v + 2 * SIDE, SIDE)


def kernel(
    slices,
    orb_ref,
    occ_ref,
    pidx_ref,
    w_hbm,
    region_ref,
    row_ref,
    col_ref,
    out_ref,
    b0,
    b1,
    b2,
    oc,
    wv,
    wg,
    acc,
    part,
    red,
    pieces,
    w_sem,
    p1s,
    p1r,
    p2s,
    p2r,
    p3s,
    p3r,
    d2s,
    d2r,
    os,
    orr,
    ods,
    odr,
    r1s,
    r1r,
    r2s,
    r2r,
    r3s,
    r3r,
):
    bufs = (b0, b1, b2)
    held = w_hbm.shape[0]
    points = w_hbm.shape[1]
    grp = lax.axis_index("grp")
    reg = lax.axis_index("reg")
    me = {"z": grp // SIDE, "x": lax.rem(grp, SIDE), "y": reg // 2}
    core = lax.rem(reg, 2)

    def device(z, x, y, c):
        return (mod4(z) * SIDE + mod4(x), mod4(y) * 2 + c)

    def near(axis, step):
        at = {k: me[k] + (step if k == axis else 0) for k in me}
        return device(at["z"], at["x"], at["y"], core)

    sibling = (grp, me["y"] * 2 + 1 - core)
    unsent = []

    def send(src, dst, ssem, rsem, to):
        copy = pltpu.make_async_remote_copy(src, dst, ssem, rsem, device_id=to, device_id_type=MESH)
        copy.start()
        unsent.append(copy)
        return copy

    barrier = pltpu.get_barrier_semaphore()
    partners = [near(axis, step) for axis in "xyz" for step in STEPS] + [sibling]
    for to in partners:
        pl.semaphore_signal(barrier, inc=1, device_id=to, device_id_type=MESH)

    w_copy = pltpu.make_async_copy(w_hbm, wv, w_sem)
    w_copy.start()

    orbs = orb_ref.shape[3]
    width = pidx_ref.shape[1]
    chosen = (
        lax.broadcasted_iota(jnp.int32, (orbs, width), 0)
        == jnp.broadcast_to(pidx_ref[...], (orbs, width))
    ).astype(jnp.bfloat16)
    start = 0
    for s, buf in enumerate(bufs):
        a1, a2, a3 = ORDERS[s]
        rows = slices[s]
        buf[core, me[a3], me[a2], me[a1]] = jnp.dot(
            orb_ref[0, 0, start : start + rows, :], chosen, preferred_element_type=jnp.float32
        ).astype(jnp.bfloat16)
        start += rows
    oc[core, me["z"], me["y"], me["x"]] = occ_ref[0, 0]

    pl.semaphore_wait(barrier, len(partners))

    def occ_step(phase):
        axis = "xyz"[phase]
        at = (core, me["z"], me["y"], me["x"])[: 4 - phase]
        block = oc.at[at]
        return [
            send(block, block, os.at[phase, i], orr.at[phase, i], near(axis, step))
            for i, step in enumerate(STEPS)
        ]

    occ_sent = occ_step(0)
    first = []
    for s, buf in enumerate(bufs):
        a1, a2, a3 = ORDERS[s]
        block = buf.at[core, me[a3], me[a2], me[a1]]
        first.append(
            [
                send(block, block, p1s.at[s, i], p1r.at[s, i], near(a1, step))
                for i, step in enumerate(STEPS)
            ]
        )

    def both(block, ssem, rsem, axis):
        return [
            send(block, block, ssem.at[i], rsem.at[i], near(axis, step))
            for i, step in enumerate((1, -1))
        ]

    mirrored = []

    def mirror(s, i3, i2, slot):
        block = bufs[s].at[core, i3, i2]
        mirrored.append(send(block, block, d2s.at[s, slot], d2r.at[s, slot], sibling))

    for copy in occ_sent:
        copy.wait_recv()
    occ_sent = occ_step(1)

    second, third = [], [[], [], []]
    for s, buf in enumerate(bufs):
        a1, a2, a3 = ORDERS[s]
        for copy in first[s]:
            copy.wait_recv()
        block = buf.at[core, me[a3], me[a2]]
        second.append(both(block, p2s.at[s], p2r.at[s], a2))
        third[s].append(both(block, p3s.at[s, 0], p3r.at[s, 0], a3))
        mirror(s, me[a3], me[a2], 0)

    for copy in occ_sent:
        copy.wait_recv()
    occ_sent = occ_step(2)

    forwards = []
    for s, buf in enumerate(bufs):
        a1, a2, a3 = ORDERS[s]
        passed = []
        for i, step in enumerate((1, -1)):
            second[s][i].wait_recv()
            j = mod4(me[a2] - step)
            half = buf.at[core, me[a3], j, pl.ds(2 * i, 2)]
            passed.append(send(half, half, p2s.at[s, 2 + i], p2r.at[s, 2 + i], near(a2, step)))
            block = buf.at[core, me[a3], j]
            third[s].append(both(block, p3s.at[s, 1 + i], p3r.at[s, 1 + i], a3))
            mirror(s, me[a3], j, 1 + i)
        forwards.append(passed)
    for s, buf in enumerate(bufs):
        a1, a2, a3 = ORDERS[s]
        for copy in forwards[s]:
            copy.wait_recv()
        j = mod4(me[a2] + 2)
        block = buf.at[core, me[a3], j]
        third[s].append(both(block, p3s.at[s, 3], p3r.at[s, 3], a3))
        mirror(s, me[a3], j, 3)

    for copy in occ_sent:
        copy.wait_recv()
    occ_side = send(oc.at[core], oc.at[core], ods, odr, sibling)
    w_copy.wait()

    def place(n, ref):
        d, g = region_ref[n, 0], ref[n]
        return lax.rem(d, 2), {"y": d // 2, "z": g // SIDE, "x": lax.rem(g, SIDE)}

    def weigh(n, carry):
        ca, pa = place(n, row_ref)
        cb, pb = place(n, col_ref)
        occ_a = oc[ca, pa["z"], pa["y"], pa["x"]]
        occ_b = oc[cb, pb["z"], pb["y"], pb["x"]]
        gram = lax.dot_general(
            occ_a, occ_b, (((0,), (0,)), ((), ())), preferred_element_type=jnp.float32
        )
        wg[n] = (gram * wv[n].astype(jnp.float32)).astype(jnp.bfloat16)
        return carry

    last = []
    for k in range(4):
        passed = []
        for s, buf in enumerate(bufs):
            a1, a2, a3 = ORDERS[s]
            j = mod4(me[a2] + (0, -1, 1, 2)[k])
            pair = []
            for i, step in enumerate((1, -1)):
                third[s][k][i].wait_recv()
                i3 = mod4(me[a3] - step)
                half = buf.at[core, i3, j, pl.ds(2 * i, 2)]
                pair.append(
                    send(half, half, p3s.at[s, k, 2 + i], p3r.at[s, k, 2 + i], near(a3, step))
                )
                mirror(s, i3, j, 4 + 3 * k + i)
            passed.append(pair)
        last.append(passed)
        if k == 0:
            occ_side.wait_recv()
        low, high = 2 * k, min(2 * k + 2, held)
        lax.fori_loop(low, high, weigh, 0)
        if k >= 1:
            for s in range(3):
                a1, a2, a3 = ORDERS[s]
                for copy in last[k - 1][s]:
                    copy.wait_recv()
                mirror(s, mod4(me[a3] + 2), mod4(me[a2] + (0, -1, 1, 2)[k - 1]), 6 + 3 * (k - 1))
    for s in range(3):
        a1, a2, a3 = ORDERS[s]
        for copy in last[3][s]:
            copy.wait_recv()
        mirror(s, mod4(me[a3] + 2), mod4(me[a2] + 2), 15)
    for copy in mirrored:
        copy.wait_recv()

    acc[...] = jnp.zeros_like(acc)

    def whole(c, at):
        return jnp.concatenate(
            [bufs[s][c, at[a3], at[a2], at[a1]] for s, (a1, a2, a3) in enumerate(ORDERS)], axis=0
        )

    def contract(n, carry):
        ca, pa = place(n, row_ref)
        cb, pb = place(n, col_ref)
        screened = jnp.dot(
            wg[n], whole(cb, pb), preferred_element_type=jnp.float32
        ).astype(jnp.bfloat16)
        term = lax.dot_general(
            whole(ca, pa), screened, (((0,), (0,)), ((), ())), preferred_element_type=jnp.float32
        )
        for c in range(2):
            for y in range(SIDE):
                hit = region_ref[n, 0] == 2 * y + c
                acc[c, y] += jnp.where(hit, term, 0.0)
        return carry

    lax.fori_loop(0, held, contract, 0)

    swap = send(acc.at[1 - core], part, r1s, r1r, sibling)
    swap.wait_recv()
    red[...] = acc[core] + part[...]

    rows = pieces.shape[1]
    sums = []
    for k in range(1, 64):
        z, x, y = mod4(me["z"] + k // 16), mod4(me["x"] + (k // 4) % 4), mod4(me["y"] + k % 4)
        piece = red.at[y, pl.ds(pl.multiple_of((z * SIDE + x) * rows, rows), rows)]
        sums.append(send(piece, pieces.at[k], r2s.at[k], r2r.at[k], device(z, x, y, core)))
    mine = pl.ds(pl.multiple_of(grp * rows, rows), rows)
    total = red[me["y"], mine]
    for k in range(1, 64):
        sums[k - 1].wait_recv()
        total = total + pieces[k]
    out_ref[0, mine] = total
    done = []
    for k in range(1, 16):
        to = device(me["z"] + k // 4, me["x"] + k % 4, me["y"], core)
        done.append(send(out_ref.at[0, mine], out_ref.at[0, mine], r3s.at[k], r3r.at[k], to))
    for copy in done:
        copy.wait_recv()
    for copy in unsent:
        copy.wait_send()


def shards(orbitals, occupied, panel_index, screening, block_region, block_row, block_col):
    held, points = screening.shape[0], screening.shape[1]
    width = panel_index.shape[0]
    tiles = points // 16
    slices = [16 * (tiles * (s + 1) // 3 - tiles * s // 3) for s in range(3)]
    occ_count = occupied.shape[2]
    vmem = pl.BlockSpec(memory_space=pltpu.VMEM)
    smem = pl.BlockSpec(memory_space=pltpu.SMEM)
    dma = pltpu.SemaphoreType.DMA
    pairs = [dma((3, 3))] * 2 + [dma((3, 4))] * 2 + [dma((3, 4, 4))] * 2 + [dma((3, 16))] * 2
    pairs += [dma((3, 3))] * 2 + [dma] * 4 + [dma((64,))] * 2 + [dma((16,))] * 2
    return pl.pallas_call(
        functools.partial(kernel, slices),
        out_shape=jax.ShapeDtypeStruct((1, width, width), jnp.float32),
        in_specs=[vmem, vmem, vmem, pl.BlockSpec(memory_space=pl.ANY), smem, smem, smem],
        out_specs=vmem,
        scratch_shapes=[
            pltpu.VMEM((2, SIDE, SIDE, SIDE, rows, width), jnp.bfloat16) for rows in slices
        ]
        + [
            pltpu.VMEM((2, SIDE, SIDE, SIDE, occ_count, points), jnp.bfloat16),
            pltpu.VMEM((held, points, points), jnp.bfloat16),
            pltpu.VMEM((held, points, points), jnp.bfloat16),
            pltpu.VMEM((2, SIDE, width, width), jnp.float32),
            pltpu.VMEM((SIDE, width, width), jnp.float32),
            pltpu.VMEM((SIDE, width, width), jnp.float32),
            pltpu.VMEM((64, width // 16, width), jnp.float32),
            dma,
        ]
        + pairs,
        compiler_params=pltpu.CompilerParams(
            collective_id=0, has_side_effects=True, vmem_limit_bytes=56 * 2**20
        ),
    )(
        orbitals,
        occupied,
        panel_index.reshape(1, width),
        screening,
        block_region,
        block_row,
        block_col,
    )


def solution(mesh):
    in_specs = (
        P("reg", "grp", None, None),
        P("reg", "grp", None, None),
        P(),
        P(("grp", "reg"), None, None),
        P(("grp", "reg"), None),
        P(("grp", "reg")),
        P(("grp", "reg")),
    )
    out_specs = P("reg", None, None)
    return jax.shard_map(shards, mesh=mesh, in_specs=in_specs, out_specs=out_specs, check_vma=False)
```

```python
import functools

import jax
import jax.numpy as jnp
from jax import lax
from jax.experimental import pallas as pl
from jax.experimental.pallas import tpu as pltpu
from jax.sharding import PartitionSpec as P

MESH = pl.DeviceIdType.MESH
SIDE = 4
ORDERS = (("x", "y", "z"), ("y", "z", "x"), ("z", "x", "y"))
STEPS = (1, -1, 2)
COPIES = 256


def mod4(v):
    return lax.rem(v + 2 * SIDE, SIDE)


def kernel(
    slices,
    orb_hbm,
    occ_hbm,
    pidx_hbm,
    w_hbm,
    region_hbm,
    row_hbm,
    col_hbm,
    out_ref,
    b0,
    b1,
    b2,
    oc,
    orb,
    pidx,
    wv,
    wg,
    acc,
    part,
    red,
    pieces,
    region,
    row,
    col,
    local_sem,
    send_sem,
    recv_sem,
):
    bufs = (b0, b1, b2)
    held = w_hbm.shape[0]
    grp = lax.axis_index("grp")
    reg = lax.axis_index("reg")
    me = {"z": grp // SIDE, "x": lax.rem(grp, SIDE), "y": reg // 2}
    core = lax.rem(reg, 2)

    def device(z, x, y, c):
        return (mod4(z) * SIDE + mod4(x), mod4(y) * 2 + c)

    def near(axis, step):
        at = {k: me[k] + (step if k == axis else 0) for k in me}
        return device(at["z"], at["x"], at["y"], core)

    sibling = (grp, me["y"] * 2 + 1 - core)
    sent = []

    def send(src, dst, to):
        n = len(sent)
        copy = pltpu.make_async_remote_copy(
            src, dst, send_sem.at[n], recv_sem.at[n], device_id=to, device_id_type=MESH
        )
        copy.start()
        sent.append(copy)
        return copy

    loads = [
        pltpu.make_async_copy(src, dst, local_sem.at[i])
        for i, (src, dst) in enumerate(
            [
                (pidx_hbm, pidx),
                (orb_hbm.at[0, 0], orb),
                (occ_hbm.at[0, 0], oc.at[0, 0, 0, 0]),
                (region_hbm, region),
                (row_hbm, row),
                (col_hbm, col),
                (w_hbm, wv),
            ]
        )
    ]
    for load in loads[:-1]:
        load.start()
    barrier = pltpu.get_barrier_semaphore()
    partners = [near(axis, step) for axis in "xyz" for step in STEPS] + [sibling]
    for to in partners:
        pl.semaphore_signal(barrier, inc=1, device_id=to, device_id_type=MESH)

    orbs = orb.shape[1]
    width = pidx.shape[1]
    loads[0].wait()
    chosen = (
        lax.broadcasted_iota(jnp.int32, (orbs, width), 0)
        == jnp.broadcast_to(pidx[...], (orbs, width))
    ).astype(jnp.bfloat16)
    loads[1].wait()
    start = 0
    for s, buf in enumerate(bufs):
        buf[0, 0, 0, 0] = jnp.dot(
            orb[start : start + slices[s], :], chosen, preferred_element_type=jnp.float32
        ).astype(jnp.bfloat16)
        start += slices[s]
    for load in loads[2:-1]:
        load.wait()
    pl.semaphore_wait(barrier, len(partners))

    def occ_step(phase):
        even, odd = "xyz"[phase], "zxy"[phase]
        copies = []
        for step in STEPS:
            at = {k: me[k] + step * ((1 - core) * (k == even) + core * (k == odd)) for k in me}
            inner = (0,) * (3 - phase)
            src = oc.at[inner + (0,)]
            dst = oc.at[inner + ((-step) % SIDE,)]
            copies.append(send(src, dst, device(at["z"], at["x"], at["y"], core)))
        return copies

    def ring(s, phase, units, *outer):
        buf, axis = bufs[s], ORDERS[s][phase - 1]
        copies = []
        for step in (1, -1):
            slot = (-step) % SIDE
            if phase == 2:
                src, dst = buf.at[0, 0, 0, units], buf.at[0, 0, slot, units]
            else:
                src, dst = buf.at[0, 0, outer[0], units], buf.at[0, slot, outer[0], units]
            copies.append(send(src, dst, near(axis, step)))
        return copies

    def pass_on(s, phase, side, units, *outer):
        buf, axis = bufs[s], ORDERS[s][phase - 1]
        step = (1, -1)[side]
        slot = (-step) % SIDE
        cut = 16 * ((slices[s] + 31) // 32)
        rows = pl.ds(0, cut) if side == 0 else pl.ds(cut, slices[s] - cut)
        if phase == 2:
            src, dst = buf.at[0, 0, slot, units, rows], buf.at[0, 0, 2, units, rows]
        else:
            src, dst = buf.at[0, slot, outer[0], units, rows], buf.at[0, 2, outer[0], units, rows]
        return send(src, dst, near(axis, step))

    mirrored = []

    def mirror(s, i3, i2):
        mirrored.append(send(bufs[s].at[0, i3, i2], bufs[s].at[1, i3, i2], sibling))

    def arrive(copies):
        for copy in copies:
            copy.wait_recv()

    own, rest, full = pl.ds(0, 1), pl.ds(1, 3), pl.ds(0, 4)
    each = range(3)

    occ_sent = occ_step(0)
    first = [
        [
            send(bufs[s].at[0, 0, 0, 0], bufs[s].at[0, 0, 0, (-step) % SIDE], near(ORDERS[s][0], step))
            for step in STEPS
        ]
        for s in each
    ]
    second_own = [ring(s, 2, own) for s in each]
    third_own = [ring(s, 3, own, 0) for s in each]
    loads[-1].start()

    arrive(occ_sent)
    occ_sent = occ_step(1)
    second_rest, third_rest = [], []
    for s in each:
        arrive(first[s])
        second_rest.append(ring(s, 2, rest))
        third_rest.append(ring(s, 3, rest, 0))
        mirror(s, 0, 0)
    arrive(occ_sent)
    occ_sent = occ_step(2)

    second_far, third_far = [[], [], []], [[], [], []]
    for s in each:
        for side in (0, 1):
            second_own[s][side].wait_recv()
            second_far[s].append(pass_on(s, 2, side, own))
            third_own[s][side].wait_recv()
            third_far[s].append(pass_on(s, 3, side, own, 0))

    third = [{}, {}, {}]
    for s in each:
        for side, slot in ((0, 3), (1, 1)):
            second_rest[s][side].wait_recv()
            second_far[s].append(pass_on(s, 2, side, rest))
            third[s][slot] = ring(s, 3, full, slot)
            mirror(s, 0, slot)
    for s in each:
        for side, slot in ((0, 3), (1, 1)):
            third_rest[s][side].wait_recv()
            third_far[s].append(pass_on(s, 3, side, rest, 0))
            mirror(s, slot, 0)
    for s in each:
        arrive(second_far[s])
        third[s][2] = ring(s, 3, full, 2)
        mirror(s, 0, 2)

    arrive(occ_sent)
    occ_side = send(oc.at[0], oc.at[1], sibling)
    loads[-1].wait()

    def place(n, ref):
        d, g = region[n], ref[n]
        parity = lax.rem(d, 2)
        at = {
            "y": mod4(d // 2 - me["y"]),
            "z": mod4(g // SIDE - me["z"]),
            "x": mod4(lax.rem(g, SIDE) - me["x"]),
        }
        return parity, lax.rem(parity + core, 2), at

    def occ_of(n, ref):
        parity, c, at = place(n, ref)
        x, y, z = at["x"], at["y"], at["z"]
        return oc[c, z + parity * (y - z), y + parity * (x - y), x + parity * (z - x)]

    def weigh(n, carry):
        gram = lax.dot_general(
            occ_of(n, row),
            occ_of(n, col),
            (((0,), (0,)), ((), ())),
            preferred_element_type=jnp.float32,
        )
        wg[n] = (gram * wv[n].astype(jnp.float32)).astype(jnp.bfloat16)
        return carry

    third_last = [[], [], []]
    for s in each:
        arrive(third_far[s])
        mirror(s, 2, 0)
    for k, j in enumerate((3, 1, 2)):
        for s in each:
            for side, slot in ((0, 3), (1, 1)):
                third[s][j][side].wait_recv()
                third_last[s].append(pass_on(s, 3, side, full, j))
                mirror(s, slot, j)
        if k == 0:
            occ_side.wait_recv()
        lax.fori_loop(3 * k, min(3 * k + 3, held), weigh, 0)
    for k, j in enumerate((3, 1, 2)):
        for s in each:
            arrive(third_last[s][2 * k : 2 * k + 2])
            mirror(s, 2, j)
    arrive(mirrored)

    acc[...] = jnp.zeros_like(acc)

    def whole(n, ref):
        _, c, at = place(n, ref)
        return jnp.concatenate(
            [bufs[s][c, at[a3], at[a2], at[a1]] for s, (a1, a2, a3) in enumerate(ORDERS)], axis=0
        )

    def contract(n, carry):
        screened = jnp.dot(
            wg[n], whole(n, col), preferred_element_type=jnp.float32
        ).astype(jnp.bfloat16)
        term = lax.dot_general(
            whole(n, row), screened, (((0,), (0,)), ((), ())), preferred_element_type=jnp.float32
        )
        for c in range(2):
            for y in range(SIDE):
                hit = region[n] == 2 * mod4(me["y"] + y) + lax.rem(core + c, 2)
                acc[c, y] += jnp.where(hit, term, 0.0)
        return carry

    lax.fori_loop(0, held, contract, 0)

    swaps = [send(acc.at[1, y], part.at[y], sibling) for y in range(SIDE)]
    rows = pieces.shape[1]
    sums = []
    for y in range(SIDE):
        swaps[y].wait_recv()
        red[y] = acc[0, y] + part[y]
        for k in range(y, 64, 4):
            if k:
                z, x = mod4(me["z"] + k // 16), mod4(me["x"] + (k // 4) % 4)
                piece = red.at[y, pl.ds(pl.multiple_of((z * SIDE + x) * rows, rows), rows)]
                sums.append(send(piece, pieces.at[k], device(z, x, me["y"] + y, core)))
    mine = pl.ds(pl.multiple_of(grp * rows, rows), rows)
    total = red[0, mine]
    arrive(sums)
    for k in range(1, 64):
        total = total + pieces[k]
    out_ref[0, mine] = total
    done = [
        send(
            out_ref.at[0, mine],
            out_ref.at[0, mine],
            device(me["z"] + k // 4, me["x"] + k % 4, me["y"], core),
        )
        for k in range(1, 16)
    ]
    arrive(done)
    for copy in sent:
        copy.wait_send()


def shards(orbitals, occupied, panel_index, screening, block_region, block_row, block_col):
    held, points = screening.shape[0], screening.shape[1]
    orbs = orbitals.shape[3]
    width = panel_index.shape[0]
    tiles = points // 16
    cuts = [0, tiles * 5 // 16, tiles * 11 // 16, tiles]
    slices = [16 * (cuts[s + 1] - cuts[s]) for s in range(3)]
    occ_count = occupied.shape[2]
    hbm = pl.BlockSpec(memory_space=pl.ANY)
    dma = pltpu.SemaphoreType.DMA
    return pl.pallas_call(
        functools.partial(kernel, slices),
        out_shape=jax.ShapeDtypeStruct((1, width, width), jnp.float32),
        in_specs=[hbm] * 7,
        out_specs=pl.BlockSpec(memory_space=pltpu.VMEM),
        scratch_shapes=[
            pltpu.VMEM((2, SIDE, SIDE, SIDE, rows, width), jnp.bfloat16) for rows in slices
        ]
        + [
            pltpu.VMEM((2, SIDE, SIDE, SIDE, occ_count, points), jnp.bfloat16),
            pltpu.VMEM((points, orbs), jnp.bfloat16),
            pltpu.VMEM((1, width), jnp.int32),
            pltpu.VMEM((held, points, points), jnp.bfloat16),
            pltpu.VMEM((held, points, points), jnp.bfloat16),
            pltpu.VMEM((2, SIDE, width, width), jnp.float32),
            pltpu.VMEM((SIDE, width, width), jnp.float32),
            pltpu.VMEM((SIDE, width, width), jnp.float32),
            pltpu.VMEM((64, width // 16, width), jnp.float32),
            pltpu.SMEM((held,), jnp.int32),
            pltpu.SMEM((held,), jnp.int32),
            pltpu.SMEM((held,), jnp.int32),
            dma((7,)),
            dma((COPIES,)),
            dma((COPIES,)),
        ],
        compiler_params=pltpu.CompilerParams(
            collective_id=0, has_side_effects=True, vmem_limit_bytes=56 * 2**20
        ),
    )(
        orbitals,
        occupied,
        panel_index.reshape(1, width),
        screening,
        block_region.reshape(held),
        block_row,
        block_col,
    )


def solution(mesh):
    in_specs = (
        P("reg", "grp", None, None),
        P("reg", "grp", None, None),
        P(),
        P(("grp", "reg"), None, None),
        P(("grp", "reg"), None),
        P(("grp", "reg")),
        P(("grp", "reg")),
    )
    out_specs = P("reg", None, None)
    return jax.shard_map(shards, mesh=mesh, in_specs=in_specs, out_specs=out_specs, check_vma=False)
```

```python
import functools

import jax
import jax.numpy as jnp
from jax import lax
from jax.experimental import pallas as pl
from jax.experimental.pallas import tpu as pltpu
from jax.sharding import PartitionSpec as P

MESH = pl.DeviceIdType.MESH
SIDE = 4
STEPS = (1, -1, 2)
COPIES = 256
SPLITS = (
    ("x", 0, "y", "z"),
    ("x", 1, "z", "y"),
    ("y", 0, "z", "x"),
    ("y", 1, "x", "z"),
    ("z", 0, "x", "y"),
    ("z", 1, "y", "x"),
)
HALF = SIDE * SIDE * 2


def mod4(v):
    return lax.rem(v + 2 * SIDE, SIDE)


def kernel(
    slices,
    orb_hbm,
    occ_hbm,
    pidx_hbm,
    w_hbm,
    region_hbm,
    row_hbm,
    col_hbm,
    out_ref,
    *scratch,
):
    count = len(SPLITS)
    bufs, packs, gots = scratch[:count], scratch[count : 2 * count], scratch[2 * count : 3 * count]
    (oc, orb, pidx, wv, wg, acc, part, red, pieces, info, infos) = scratch[3 * count : 3 * count + 11]
    (region, row, col, infos_s, mine_at, pack_at) = scratch[3 * count + 11 : 3 * count + 17]
    local_sem, info_sem, send_sem, recv_sem = scratch[3 * count + 17 :]
    held = w_hbm.shape[0]
    grp = lax.axis_index("grp")
    reg = lax.axis_index("reg")
    me = {"z": grp // SIDE, "x": lax.rem(grp, SIDE), "y": reg // 2}
    core = lax.rem(reg, 2)

    def device(z, x, y, c):
        return (mod4(z) * SIDE + mod4(x), mod4(y) * 2 + c)

    def near(axis, step):
        at = {k: me[k] + (step if k == axis else 0) for k in me}
        return device(at["z"], at["x"], at["y"], core)

    sibling = (grp, me["y"] * 2 + 1 - core)
    sent = []

    def send(src, dst, to):
        n = len(sent)
        copy = pltpu.make_async_remote_copy(
            src, dst, send_sem.at[n], recv_sem.at[n], device_id=to, device_id_type=MESH
        )
        copy.start()
        sent.append(copy)
        return copy

    loads = [
        pltpu.make_async_copy(src, dst, local_sem.at[i])
        for i, (src, dst) in enumerate(
            [
                (pidx_hbm, pidx),
                (orb_hbm.at[0, 0], orb),
                (occ_hbm.at[0, 0], oc.at[0, 0, 0, 0]),
                (region_hbm, region),
                (row_hbm, row),
                (col_hbm, col),
                (w_hbm, wv),
            ]
        )
    ]
    for load in loads[:-1]:
        load.start()
    barrier = pltpu.get_barrier_semaphore()
    partners = [near(axis, step) for axis in "xyz" for step in STEPS] + [sibling]
    for to in partners:
        pl.semaphore_signal(barrier, inc=1, device_id=to, device_id_type=MESH)

    orbs = orb.shape[1]
    width = pidx.shape[1]
    loads[0].wait()
    chosen = (
        lax.broadcasted_iota(jnp.int32, (orbs, width), 0)
        == jnp.broadcast_to(pidx[...], (orbs, width))
    ).astype(jnp.bfloat16)
    loads[1].wait()
    start = 0
    for s, buf in enumerate(bufs):
        buf[0] = jnp.dot(
            orb[start : start + slices[s], :], chosen, preferred_element_type=jnp.float32
        ).astype(jnp.bfloat16)
        start += slices[s]
    for load in loads[2:-1]:
        load.wait()
    sub = lax.broadcasted_iota(jnp.int32, info.shape, 0)
    lane = lax.broadcasted_iota(jnp.int32, info.shape, 1)
    held_info = jnp.zeros(info.shape, jnp.int32)
    for i, ref in enumerate((region, row, col)):
        for n in range(held):
            held_info = jnp.where((sub == i) & (lane == n), ref[n], held_info)
    info[...] = held_info
    pl.semaphore_wait(barrier, len(partners))

    def occ_step(phase):
        even, odd = "xyz"[phase], "zxy"[phase]
        copies = []
        for step in STEPS:
            at = {k: me[k] + step * ((1 - core) * (k == even) + core * (k == odd)) for k in me}
            inner = (0,) * (3 - phase)
            src = oc.at[inner + (0,)]
            dst = oc.at[inner + ((-step) % SIDE,)]
            copies.append(send(src, dst, device(at["z"], at["x"], at["y"], core)))
        return copies

    toward = [(1 - 2 * lax.rem(me[a], 2)) * (1 - 2 * pairing) for a, pairing, _, _ in SPLITS]
    each = range(count)

    def spread(s, t):
        buf, axis = bufs[s], SPLITS[s][2]
        return [send(buf.at[t], buf.at[2 * ((-step) % SIDE) + t], near(axis, step)) for step in STEPS]

    def group(s, low, size):
        buf, axis = bufs[s], SPLITS[s][3]
        return [
            send(
                buf.at[pl.ds(low, size)],
                buf.at[pl.ds(2 * SIDE * ((-step) % SIDE) + low, size)],
                near(axis, step),
            )
            for step in (1, -1)
        ]

    def pass_on(s, side, low, size):
        buf, axis = bufs[s], SPLITS[s][3]
        step = (1, -1)[side]
        low, size = low + side * size // 2, size // 2
        return send(
            buf.at[pl.ds(2 * SIDE * ((-step) % SIDE) + low, size)],
            buf.at[pl.ds(2 * SIDE * 2 + low, size)],
            near(axis, step),
        )

    def mirror(s, c):
        low = 2 * SIDE * c
        return send(
            bufs[s].at[pl.ds(low, 2 * SIDE)], bufs[s].at[pl.ds(HALF + low, 2 * SIDE)], sibling
        )

    def arrive(copies):
        for copy in copies:
            copy.wait_recv()

    swapped = [
        send(bufs[s].at[0], bufs[s].at[1], near(SPLITS[s][0], -toward[s])) for s in each
    ]
    occ_sent = occ_step(0)
    own = [spread(s, 0) for s in each]
    told = [send(info, infos.at[s], near(SPLITS[s][0], toward[s])) for s in each]
    loads[-1].start()

    arrive(occ_sent)
    occ_sent = occ_step(1)
    other, near_groups = [], []
    for s in each:
        swapped[s].wait_recv()
        other.append(spread(s, 1))
        near_groups.append(group(s, 0, 2))
    arrive(occ_sent)
    occ_sent = occ_step(2)

    def distance(d, g):
        parity = lax.rem(d, 2)
        at = {
            "y": mod4(d // 2 - me["y"]),
            "z": mod4(g // SIDE - me["z"]),
            "x": mod4(lax.rem(g, SIDE) - me["x"]),
        }
        return parity, lax.rem(parity + core, 2), at

    def gathered(s, c, at):
        _, _, axis_b, axis_c = SPLITS[s]
        return ((c * SIDE + at[axis_c]) * SIDE + at[axis_b]) * 2

    def find(n, carry):
        for i, ref in enumerate((row, col)):
            _, c, at = distance(region[n], ref[n])
            for s in each:
                along, base = at[SPLITS[s][0]], gathered(s, c, at)
                mine_at[s, 2 * n + i] = jnp.where(
                    along == 0,
                    base,
                    jnp.where(along == 2 + toward[s], base + 1, -1),
                )
        return carry

    lax.fori_loop(0, held, find, 0)

    far_groups, mirrored = [], [[] for s in each]
    for s in each:
        arrive(own[s])
        arrive(other[s])
        far_groups.append(group(s, 2, 2 * SIDE - 2))
        mirrored[s].append(mirror(s, 0))
    passed = [[] for s in each]
    for s in each:
        for side in (0, 1):
            near_groups[s][side].wait_recv()
            passed[s].append(pass_on(s, side, 0, 2))

    arrive(told)
    info_loads = [
        pltpu.make_async_copy(infos.at[s], infos_s.at[s], info_sem.at[s]) for s in each
    ]
    for load in info_loads:
        load.start()
    for load in info_loads:
        load.wait()

    def plan(n, carry):
        for s in each:
            for i in range(2):
                _, c, at = distance(infos_s[s, 0, n], infos_s[s, 1 + i, n])
                base = gathered(s, c, at)
                pack_at[s, 2 * n + i] = jnp.where(at[SPLITS[s][0]] == 0, base, base + 1)
        return carry

    lax.fori_loop(0, held, plan, 0)
    arrive(occ_sent)
    occ_side = send(oc.at[0], oc.at[1], sibling)

    for s in each:
        for side, slot in ((0, 3), (1, 1)):
            far_groups[s][side].wait_recv()
            passed[s].append(pass_on(s, side, 2, 2 * SIDE - 2))
            mirrored[s].append(mirror(s, slot))
    for s in each:
        arrive(passed[s])
        mirrored[s].append(mirror(s, 2))
    fetched = []
    for s in each:
        arrive(mirrored[s])
        for i in range(2 * held):
            packs[s][i] = bufs[s][pack_at[s, i]]
        fetched.append(
            send(
                packs[s],
                gots[s],
                near(SPLITS[s][0], toward[s]),
            )
        )

    occ_side.wait_recv()
    loads[-1].wait()

    def occ_of(n, ref):
        parity, c, at = distance(region[n], ref[n])
        x, y, z = at["x"], at["y"], at["z"]
        return oc[c, z + parity * (y - z), y + parity * (x - y), x + parity * (z - x)]

    def weigh(n, carry):
        gram = lax.dot_general(
            occ_of(n, row),
            occ_of(n, col),
            (((0,), (0,)), ((), ())),
            preferred_element_type=jnp.float32,
        )
        wg[n] = (gram * wv[n].astype(jnp.float32)).astype(jnp.bfloat16)
        return carry

    lax.fori_loop(0, held, weigh, 0)
    arrive(fetched)

    acc[...] = jnp.zeros_like(acc)

    def whole(n, i):
        parts = []
        for s in each:
            at = mine_at[s, 2 * n + i]
            parts.append(jnp.where(at >= 0, bufs[s][jnp.maximum(at, 0)], gots[s][2 * n + i]))
        return jnp.concatenate(parts, axis=0)

    def contract(n, carry):
        screened = jnp.dot(
            wg[n], whole(n, 1), preferred_element_type=jnp.float32
        ).astype(jnp.bfloat16)
        term = lax.dot_general(
            whole(n, 0), screened, (((0,), (0,)), ((), ())), preferred_element_type=jnp.float32
        )
        for c in range(2):
            for y in range(SIDE):
                hit = region[n] == 2 * mod4(me["y"] + y) + lax.rem(core + c, 2)
                acc[c, y] += jnp.where(hit, term, 0.0)
        return carry

    for n in range(held):
        contract(n, 0)

    swaps = {y: send(acc.at[1, y], part.at[y], sibling) for y in (2, 1, 3, 0)}
    far = lambda k: -sum(min(v, SIDE - v) for v in (k // 16, (k // 4) % 4, k % 4))
    rows = pieces.shape[1]
    sums = []
    for y in swaps:
        swaps[y].wait_recv()
        red[y] = acc[0, y] + part[y]
        for k in sorted(range(y, 64, 4), key=far):
            if k:
                z, x = mod4(me["z"] + k // 16), mod4(me["x"] + (k // 4) % 4)
                piece = red.at[y, pl.ds(pl.multiple_of((z * SIDE + x) * rows, rows), rows)]
                sums.append(send(piece, pieces.at[k], device(z, x, me["y"] + y, core)))
    mine = pl.ds(pl.multiple_of(grp * rows, rows), rows)
    total = red[0, mine]
    arrive(sums)
    for k in range(1, 64):
        total = total + pieces[k]
    out_ref[0, mine] = total
    done = [
        send(
            out_ref.at[0, mine],
            out_ref.at[0, mine],
            device(me["z"] + k // 4, me["x"] + k % 4, me["y"], core),
        )
        for k in sorted(range(1, 16), key=far)
    ]
    arrive(done)
    for copy in sent:
        copy.wait_send()


def shards(orbitals, occupied, panel_index, screening, block_region, block_row, block_col):
    held, points = screening.shape[0], screening.shape[1]
    orbs = orbitals.shape[3]
    width = panel_index.shape[0]
    tiles, count = points // 16, len(SPLITS)
    cuts = [(tiles * s + count - 1) // count for s in range(count + 1)]
    slices = [16 * (cuts[s + 1] - cuts[s]) for s in range(count)]
    occ_count = occupied.shape[2]
    hbm = pl.BlockSpec(memory_space=pl.ANY)
    dma = pltpu.SemaphoreType.DMA
    return pl.pallas_call(
        functools.partial(kernel, slices),
        out_shape=jax.ShapeDtypeStruct((1, width, width), jnp.float32),
        in_specs=[hbm] * 7,
        out_specs=pl.BlockSpec(memory_space=pltpu.VMEM),
        scratch_shapes=[
            pltpu.VMEM((2 * HALF, rows, width), jnp.bfloat16) for rows in slices
        ]
        + [pltpu.VMEM((2 * held, rows, width), jnp.bfloat16) for rows in slices] * 2
        + [
            pltpu.VMEM((2, SIDE, SIDE, SIDE, occ_count, points), jnp.bfloat16),
            pltpu.VMEM((points, orbs), jnp.bfloat16),
            pltpu.VMEM((1, width), jnp.int32),
            pltpu.VMEM((held, points, points), jnp.bfloat16),
            pltpu.VMEM((held, points, points), jnp.bfloat16),
            pltpu.VMEM((2, SIDE, width, width), jnp.float32),
            pltpu.VMEM((SIDE, width, width), jnp.float32),
            pltpu.VMEM((SIDE, width, width), jnp.float32),
            pltpu.VMEM((64, width // 16, width), jnp.float32),
            pltpu.VMEM((8, 128), jnp.int32),
            pltpu.VMEM((count, 8, 128), jnp.int32),
            pltpu.SMEM((held,), jnp.int32),
            pltpu.SMEM((held,), jnp.int32),
            pltpu.SMEM((held,), jnp.int32),
            pltpu.SMEM((count, 8, 128), jnp.int32),
            pltpu.SMEM((count, 2 * held), jnp.int32),
            pltpu.SMEM((count, 2 * held), jnp.int32),
            dma((7,)),
            dma((count,)),
            dma((COPIES,)),
            dma((COPIES,)),
        ],
        compiler_params=pltpu.CompilerParams(
            collective_id=0, has_side_effects=True, vmem_limit_bytes=56 * 2**20
        ),
    )(
        orbitals,
        occupied,
        panel_index.reshape(1, width),
        screening,
        block_region.reshape(held),
        block_row,
        block_col,
    )


def solution(mesh):
    in_specs = (
        P("reg", "grp", None, None),
        P("reg", "grp", None, None),
        P(),
        P(("grp", "reg"), None, None),
        P(("grp", "reg"), None),
        P(("grp", "reg")),
        P(("grp", "reg")),
    )
    out_specs = P("reg", None, None)
    return jax.shard_map(shards, mesh=mesh, in_specs=in_specs, out_specs=out_specs, check_vma=False)
```

```python
import functools

import jax
import jax.numpy as jnp
from jax import lax
from jax.experimental import pallas as pl
from jax.experimental.pallas import tpu as pltpu
from jax.sharding import PartitionSpec as P

MESH = pl.DeviceIdType.MESH
SIDE = 4
COPIES = 256
SPLITS = (("x", "y", "z"), ("y", "z", "x"), ("z", "x", "y"))
HALF = SIDE * SIDE * 2


def mod4(v):
    return lax.rem(v + 2 * SIDE, SIDE)


def kernel(
    slices,
    orb_hbm,
    occ_hbm,
    pidx_hbm,
    w_hbm,
    region_hbm,
    row_hbm,
    col_hbm,
    out_ref,
    *scratch,
):
    count = len(SPLITS)
    bufs, packs, gots = scratch[:count], scratch[count : 3 * count], scratch[3 * count : 5 * count]
    (oc, orb, pidx, wv, wg, acc, part, red, pieces, info, infos) = scratch[5 * count : 5 * count + 11]
    (region, row, col, infos_s, mine_at, pack_at) = scratch[5 * count + 11 : 5 * count + 17]
    local_sem, info_sem, send_sem, recv_sem = scratch[5 * count + 17 :]
    held = w_hbm.shape[0]
    grp = lax.axis_index("grp")
    reg = lax.axis_index("reg")
    me = {"z": grp // SIDE, "x": lax.rem(grp, SIDE), "y": reg // 2}
    core = lax.rem(reg, 2)

    def device(z, x, y, c):
        return (mod4(z) * SIDE + mod4(x), mod4(y) * 2 + c)

    def near(axis, step):
        at = {k: me[k] + (step if k == axis else 0) for k in me}
        return device(at["z"], at["x"], at["y"], core)

    sibling = (grp, me["y"] * 2 + 1 - core)
    sent = []

    def send(src, dst, to):
        n = len(sent)
        copy = pltpu.make_async_remote_copy(
            src, dst, send_sem.at[n], recv_sem.at[n], device_id=to, device_id_type=MESH
        )
        copy.start()
        sent.append(copy)
        return copy

    loads = [
        pltpu.make_async_copy(src, dst, local_sem.at[i])
        for i, (src, dst) in enumerate(
            [
                (pidx_hbm, pidx),
                (orb_hbm.at[0, 0], orb),
                (occ_hbm.at[0, 0], oc.at[0, 0, 0, 0]),
                (region_hbm, region),
                (row_hbm, row),
                (col_hbm, col),
                (w_hbm, wv),
            ]
        )
    ]
    for load in loads[:-1]:
        load.start()
    barrier = pltpu.get_barrier_semaphore()
    partners = [near(axis, step) for axis in "xyz" for step in (1, -1)] + [sibling]
    for to in partners:
        pl.semaphore_signal(barrier, inc=1, device_id=to, device_id_type=MESH)

    orbs = orb.shape[1]
    width = pidx.shape[1]
    loads[0].wait()
    chosen = (
        lax.broadcasted_iota(jnp.int32, (orbs, width), 0)
        == jnp.broadcast_to(pidx[...], (orbs, width))
    ).astype(jnp.bfloat16)
    loads[1].wait()
    start = 0
    for s, buf in enumerate(bufs):
        buf[0] = jnp.dot(
            orb[start : start + slices[s], :], chosen, preferred_element_type=jnp.float32
        ).astype(jnp.bfloat16)
        start += slices[s]
    for load in loads[2:-1]:
        load.wait()
    sub = lax.broadcasted_iota(jnp.int32, info.shape, 0)
    lane = lax.broadcasted_iota(jnp.int32, info.shape, 1)
    held_info = jnp.zeros(info.shape, jnp.int32)
    for i, ref in enumerate((region, row, col)):
        for n in range(held):
            held_info = jnp.where((sub == i) & (lane == n), ref[n], held_info)
    info[...] = held_info
    pl.semaphore_wait(barrier, len(partners))

    def occ_to(phase, step):
        even, odd = "xyz"[phase], "zxy"[phase]
        at = {k: me[k] + step * ((1 - core) * (k == even) + core * (k == odd)) for k in me}
        return device(at["z"], at["x"], at["y"], core)

    def occ_step(phase):
        inner = (0,) * (3 - phase)
        return [
            send(oc.at[inner + (0,)], oc.at[inner + ((-step) % SIDE,)], occ_to(phase, step))
            for step in (1, -1)
        ]

    def occ_pass(phase):
        inner = (0,) * (3 - phase)
        copies = []
        for side, step in enumerate((1, -1)):
            if phase == 0 and side == 1:
                continue
            half = (pl.ds(2 * side, 2),) if phase else ()
            src = oc.at[inner + ((-step) % SIDE,) + half]
            dst = oc.at[inner + (2,) + half]
            copies.append(send(src, dst, occ_to(phase, step)))
        return copies

    each = range(count)
    ways = [(s, way) for s in each for way in (0, 1)]
    toward = [
        (1 - 2 * lax.rem(me[SPLITS[s][0]], 2)) * (1 - 2 * way) for s, way in ways
    ]
    cuts = [16 * ((rows + 31) // 32) for rows in slices]
    halves = [
        pl.ds(0, cuts[s]) if way == 0 else pl.ds(cuts[s], slices[s] - cuts[s]) for s, way in ways
    ]

    def spread(s, t, size, steps):
        buf, axis = bufs[s], SPLITS[s][1]
        return [
            send(
                buf.at[pl.ds(t, size)],
                buf.at[pl.ds(2 * ((-step) % SIDE) + t, size)],
                near(axis, step),
            )
            for step in steps
        ]

    def group(s, low, size):
        buf, axis = bufs[s], SPLITS[s][2]
        return [
            send(
                buf.at[pl.ds(low, size)],
                buf.at[pl.ds(2 * SIDE * ((-step) % SIDE) + low, size)],
                near(axis, step),
            )
            for step in (1, -1)
        ]

    def pass_on(s, side, low, size):
        buf, axis = bufs[s], SPLITS[s][2]
        step = (1, -1)[side]
        low, size = low + side * size // 2, size // 2
        return send(
            buf.at[pl.ds(2 * SIDE * ((-step) % SIDE) + low, size)],
            buf.at[pl.ds(2 * SIDE * 2 + low, size)],
            near(axis, step),
        )

    def mirror(s, c):
        low = 2 * SIDE * c
        return send(
            bufs[s].at[pl.ds(low, 2 * SIDE)], bufs[s].at[pl.ds(HALF + low, 2 * SIDE)], sibling
        )

    def arrive(copies):
        for copy in copies:
            copy.wait_recv()

    swapped = [
        send(bufs[s].at[0, halves[w]], bufs[s].at[1, halves[w]], near(SPLITS[s][0], -toward[w]))
        for w, (s, way) in enumerate(ways)
    ]
    own = [spread(s, 0, 1, (1, -1)) for s in each]
    occ_sent = occ_step(0)
    told = [
        send(info, infos.at[w], near(SPLITS[s][0], toward[w])) for w, (s, way) in enumerate(ways)
    ]
    loads[-1].start()

    other, near_groups = [], []
    for s in each:
        arrive(own[s])
        arrive(swapped[2 * s : 2 * s + 2])
        other.append(spread(s, 1, 1, (1, -1)) + spread(s, 0, 2, (2,)))
        near_groups.append(group(s, 0, 2))
    arrive(occ_sent)
    occ_sent = occ_pass(0)

    def distance(d, g):
        parity = lax.rem(d, 2)
        at = {
            "y": mod4(d // 2 - me["y"]),
            "z": mod4(g // SIDE - me["z"]),
            "x": mod4(lax.rem(g, SIDE) - me["x"]),
        }
        return parity, lax.rem(parity + core, 2), at

    def gathered(s, c, at):
        _, axis_b, axis_c = SPLITS[s]
        return ((c * SIDE + at[axis_c]) * SIDE + at[axis_b]) * 2

    def find(n, carry):
        for i, ref in enumerate((row, col)):
            _, c, at = distance(region[n], ref[n])
            for w, (s, way) in enumerate(ways):
                along, base = at[SPLITS[s][0]], gathered(s, c, at)
                mine_at[w, 2 * n + i] = jnp.where(
                    along == 0,
                    base,
                    jnp.where(along == 2 + toward[w], base + 1, -1),
                )
        return carry

    lax.fori_loop(0, held, find, 0)

    far_groups, mirrored = [], [[] for s in each]
    for s in each:
        arrive(other[s])
        far_groups.append(group(s, 2, 2 * SIDE - 2))
        mirrored[s].append(mirror(s, 0))
    passed = [[] for s in each]
    for s in each:
        for side in (0, 1):
            near_groups[s][side].wait_recv()
            passed[s].append(pass_on(s, side, 0, 2))
    arrive(occ_sent)
    occ_sent = occ_step(1)

    arrive(told)
    info_loads = [
        pltpu.make_async_copy(infos.at[w], infos_s.at[w], info_sem.at[w]) for w in range(2 * count)
    ]
    for load in info_loads:
        load.start()
    for load in info_loads:
        load.wait()

    def plan(n, carry):
        for w, (s, way) in enumerate(ways):
            for i in range(2):
                _, c, at = distance(infos_s[w, 0, n], infos_s[w, 1 + i, n])
                base = gathered(s, c, at)
                pack_at[w, 2 * n + i] = jnp.where(at[SPLITS[s][0]] == 0, base, base + 1)
        return carry

    lax.fori_loop(0, held, plan, 0)
    arrive(occ_sent)
    occ_sent = occ_pass(1)

    for s in each:
        for side, slot in ((0, 3), (1, 1)):
            far_groups[s][side].wait_recv()
            passed[s].append(pass_on(s, side, 2, 2 * SIDE - 2))
            mirrored[s].append(mirror(s, slot))
    arrive(occ_sent)
    occ_sent = occ_step(2)
    for s in each:
        arrive(passed[s])
        mirrored[s].append(mirror(s, 2))
    arrive(occ_sent)
    occ_sent = occ_pass(2)
    fetched = []
    for w, (s, way) in enumerate(ways):
        if way == 0:
            arrive(mirrored[s])
        for i in range(2 * held):
            packs[w][i] = bufs[s][pack_at[w, i], halves[w]]
        fetched.append(send(packs[w], gots[w], near(SPLITS[s][0], toward[w])))
    arrive(occ_sent)
    occ_side = send(oc.at[0], oc.at[1], sibling)

    occ_side.wait_recv()
    loads[-1].wait()

    def occ_of(n, ref):
        parity, c, at = distance(region[n], ref[n])
        x, y, z = at["x"], at["y"], at["z"]
        return oc[c, z + parity * (y - z), y + parity * (x - y), x + parity * (z - x)]

    def weigh(n, carry):
        gram = lax.dot_general(
            occ_of(n, row),
            occ_of(n, col),
            (((0,), (0,)), ((), ())),
            preferred_element_type=jnp.float32,
        )
        wg[n] = (gram * wv[n].astype(jnp.float32)).astype(jnp.bfloat16)
        return carry

    lax.fori_loop(0, held, weigh, 0)
    arrive(fetched)

    acc[...] = jnp.zeros_like(acc)

    def whole(n, i):
        parts = []
        for w, (s, way) in enumerate(ways):
            at = mine_at[w, 2 * n + i]
            mine = bufs[s][jnp.maximum(at, 0), halves[w]]
            parts.append(jnp.where(at >= 0, mine, gots[w][2 * n + i]))
        return jnp.concatenate(parts, axis=0)

    def contract(n, carry):
        screened = jnp.dot(
            wg[n], whole(n, 1), preferred_element_type=jnp.float32
        ).astype(jnp.bfloat16)
        term = lax.dot_general(
            whole(n, 0), screened, (((0,), (0,)), ((), ())), preferred_element_type=jnp.float32
        )
        for c in range(2):
            for y in range(SIDE):
                hit = region[n] == 2 * mod4(me["y"] + y) + lax.rem(core + c, 2)
                acc[c, y] += jnp.where(hit, term, 0.0)
        return carry

    for n in range(held):
        contract(n, 0)

    swaps = {y: send(acc.at[1, y], part.at[y], sibling) for y in (2, 1, 3, 0)}
    far = lambda k: -sum(min(v, SIDE - v) for v in (k // 16, (k // 4) % 4, k % 4))
    rows = pieces.shape[1]
    sums = []
    for y in swaps:
        swaps[y].wait_recv()
        red[y] = acc[0, y] + part[y]
        for k in sorted(range(y, 64, 4), key=far):
            if k:
                z, x = mod4(me["z"] + k // 16), mod4(me["x"] + (k // 4) % 4)
                piece = red.at[y, pl.ds(pl.multiple_of((z * SIDE + x) * rows, rows), rows)]
                sums.append(send(piece, pieces.at[k], device(z, x, me["y"] + y, core)))
    mine = pl.ds(pl.multiple_of(grp * rows, rows), rows)
    total = red[0, mine]
    arrive(sums)
    for k in range(1, 64):
        total = total + pieces[k]
    out_ref[0, mine] = total
    done = [
        send(
            out_ref.at[0, mine],
            out_ref.at[0, mine],
            device(me["z"] + k // 4, me["x"] + k % 4, me["y"], core),
        )
        for k in sorted(range(1, 16), key=far)
    ]
    arrive(done)
    for copy in sent:
        copy.wait_send()


def shards(orbitals, occupied, panel_index, screening, block_region, block_row, block_col):
    held, points = screening.shape[0], screening.shape[1]
    orbs = orbitals.shape[3]
    width = panel_index.shape[0]
    tiles, count = points // 16, len(SPLITS)
    cuts = [0, tiles * 5 // 16, tiles * 11 // 16, tiles]
    slices = [16 * (cuts[s + 1] - cuts[s]) for s in range(count)]
    halves = []
    for rows in slices:
        halves += [16 * ((rows + 31) // 32), rows - 16 * ((rows + 31) // 32)]
    occ_count = occupied.shape[2]
    hbm = pl.BlockSpec(memory_space=pl.ANY)
    dma = pltpu.SemaphoreType.DMA
    return pl.pallas_call(
        functools.partial(kernel, slices),
        out_shape=jax.ShapeDtypeStruct((1, width, width), jnp.float32),
        in_specs=[hbm] * 7,
        out_specs=pl.BlockSpec(memory_space=pltpu.VMEM),
        scratch_shapes=[
            pltpu.VMEM((2 * HALF, rows, width), jnp.bfloat16) for rows in slices
        ]
        + [pltpu.VMEM((2 * held, rows, width), jnp.bfloat16) for rows in halves] * 2
        + [
            pltpu.VMEM((2, SIDE, SIDE, SIDE, occ_count, points), jnp.bfloat16),
            pltpu.VMEM((points, orbs), jnp.bfloat16),
            pltpu.VMEM((1, width), jnp.int32),
            pltpu.VMEM((held, points, points), jnp.bfloat16),
            pltpu.VMEM((held, points, points), jnp.bfloat16),
            pltpu.VMEM((2, SIDE, width, width), jnp.float32),
            pltpu.VMEM((SIDE, width, width), jnp.float32),
            pltpu.VMEM((SIDE, width, width), jnp.float32),
            pltpu.VMEM((64, width // 16, width), jnp.float32),
            pltpu.VMEM((8, 128), jnp.int32),
            pltpu.VMEM((2 * count, 8, 128), jnp.int32),
            pltpu.SMEM((held,), jnp.int32),
            pltpu.SMEM((held,), jnp.int32),
            pltpu.SMEM((held,), jnp.int32),
            pltpu.SMEM((2 * count, 8, 128), jnp.int32),
            pltpu.SMEM((2 * count, 2 * held), jnp.int32),
            pltpu.SMEM((2 * count, 2 * held), jnp.int32),
            dma((7,)),
            dma((2 * count,)),
            dma((COPIES,)),
            dma((COPIES,)),
        ],
        compiler_params=pltpu.CompilerParams(
            collective_id=0, has_side_effects=True, vmem_limit_bytes=56 * 2**20
        ),
    )(
        orbitals,
        occupied,
        panel_index.reshape(1, width),
        screening,
        block_region.reshape(held),
        block_row,
        block_col,
    )


def solution(mesh):
    in_specs = (
        P("reg", "grp", None, None),
        P("reg", "grp", None, None),
        P(),
        P(("grp", "reg"), None, None),
        P(("grp", "reg"), None),
        P(("grp", "reg")),
        P(("grp", "reg")),
    )
    out_specs = P("reg", None, None)
    return jax.shard_map(shards, mesh=mesh, in_specs=in_specs, out_specs=out_specs, check_vma=False)
```

```python
import functools

import jax
import jax.numpy as jnp
from jax import lax
from jax.experimental import pallas as pl
from jax.experimental.pallas import tpu as pltpu
from jax.sharding import PartitionSpec as P

MESH = pl.DeviceIdType.MESH
SIDE = 4
COPIES = 256
SPLITS = (("x", "y", "z"), ("y", "z", "x"), ("z", "x", "y"))
PLACE = {1: 2, -1: 1, 2: 3}
HALF = SIDE * SIDE * 2


def mod4(v):
    return lax.rem(v + 2 * SIDE, SIDE)


def kernel(
    slices,
    orb_hbm,
    occ_hbm,
    pidx_hbm,
    w_hbm,
    region_hbm,
    row_hbm,
    col_hbm,
    out_ref,
    *scratch,
):
    count = len(SPLITS)
    bufs, packs, gots = scratch[:count], scratch[count : 3 * count], scratch[3 * count : 5 * count]
    (oc, orb, pidx, wv, wg, acc, part, red, pieces, info, infos) = scratch[5 * count : 5 * count + 11]
    (region, row, col, infos_s, mine_at, pack_at) = scratch[5 * count + 11 : 5 * count + 17]
    local_sem, info_sem, send_sem, recv_sem = scratch[5 * count + 17 :]
    held = w_hbm.shape[0]
    grp = lax.axis_index("grp")
    reg = lax.axis_index("reg")
    me = {"z": grp // SIDE, "x": lax.rem(grp, SIDE), "y": reg // 2}
    core = lax.rem(reg, 2)

    def device(z, x, y, c):
        return (mod4(z) * SIDE + mod4(x), mod4(y) * 2 + c)

    def near(axis, step):
        at = {k: me[k] + (step if k == axis else 0) for k in me}
        return device(at["z"], at["x"], at["y"], core)

    sibling = (grp, me["y"] * 2 + 1 - core)
    sent = []

    def send(src, dst, to):
        n = len(sent)
        copy = pltpu.make_async_remote_copy(
            src, dst, send_sem.at[n], recv_sem.at[n], device_id=to, device_id_type=MESH
        )
        copy.start()
        sent.append(copy)
        return copy

    loads = [
        pltpu.make_async_copy(src, dst, local_sem.at[i])
        for i, (src, dst) in enumerate(
            [
                (pidx_hbm, pidx),
                (orb_hbm.at[0, 0], orb),
                (occ_hbm.at[0, 0], oc.at[0, 0, 0, 0]),
                (region_hbm, region),
                (row_hbm, row),
                (col_hbm, col),
                (w_hbm, wv),
            ]
        )
    ]
    for load in loads[:-1]:
        load.start()
    barrier = pltpu.get_barrier_semaphore()
    partners = [near(axis, step) for axis in "xyz" for step in (1, -1)] + [sibling]
    for to in partners:
        pl.semaphore_signal(barrier, inc=1, device_id=to, device_id_type=MESH)

    orbs = orb.shape[1]
    width = pidx.shape[1]
    loads[0].wait()
    chosen = (
        lax.broadcasted_iota(jnp.int32, (orbs, width), 0)
        == jnp.broadcast_to(pidx[...], (orbs, width))
    ).astype(jnp.bfloat16)
    loads[1].wait()
    start = 0
    for s, buf in enumerate(bufs):
        buf[0] = jnp.dot(
            orb[start : start + slices[s], :], chosen, preferred_element_type=jnp.float32
        ).astype(jnp.bfloat16)
        start += slices[s]
    for load in loads[2:-1]:
        load.wait()
    sub = lax.broadcasted_iota(jnp.int32, info.shape, 0)
    lane = lax.broadcasted_iota(jnp.int32, info.shape, 1)
    held_info = jnp.zeros(info.shape, jnp.int32)
    for i, ref in enumerate((region, row, col)):
        for n in range(held):
            held_info = jnp.where((sub == i) & (lane == n), ref[n], held_info)
    info[...] = held_info
    pl.semaphore_wait(barrier, len(partners))

    def occ_to(phase, step):
        even, odd = "xyz"[phase], "zxy"[phase]
        at = {k: me[k] + step * ((1 - core) * (k == even) + core * (k == odd)) for k in me}
        return device(at["z"], at["x"], at["y"], core)

    def occ_step(phase, steps):
        inner = (0,) * (3 - phase)
        return [
            send(oc.at[inner + (0,)], oc.at[inner + ((-step) % SIDE,)], occ_to(phase, step))
            for step in steps
        ]

    each = range(count)
    ways = [(s, way) for s in each for way in (0, 1)]
    toward = [(1 - 2 * lax.rem(me[SPLITS[s][0]], 2)) * (1 - 2 * way) for s, way in ways]
    cuts = [16 * ((rows + 31) // 32) for rows in slices]
    halves = [
        pl.ds(0, cuts[s]) if way == 0 else pl.ds(cuts[s], slices[s] - cuts[s]) for s, way in ways
    ]
    unit = 2 * SIDE

    def spread(s, t, size, steps):
        buf, axis = bufs[s], SPLITS[s][1]
        return [
            send(
                buf.at[pl.ds(t, size)],
                buf.at[pl.ds(2 * PLACE[step] + t, size)],
                near(axis, step),
            )
            for step in steps
        ]

    def group(s, low, size):
        buf, axis = bufs[s], SPLITS[s][2]
        return [
            send(
                buf.at[pl.ds(low, size)],
                buf.at[pl.ds(unit * PLACE[step] + low, size)],
                near(axis, step),
            )
            for step in (1, -1)
        ]

    def pass_on(s, side, low, size):
        buf, axis = bufs[s], SPLITS[s][2]
        step = (1, -1)[side]
        low, size = low + side * size // 2, size // 2
        return send(
            buf.at[pl.ds(unit * PLACE[step] + low, size)],
            buf.at[pl.ds(unit * PLACE[2] + low, size)],
            near(axis, step),
        )

    def mirror(s, low, size):
        buf = bufs[s]
        return send(buf.at[pl.ds(low, size)], buf.at[pl.ds(HALF + low, size)], sibling)

    def arrive(copies):
        for copy in copies:
            copy.wait_recv()

    passed, mirrored = [[] for s in each], [[] for s in each]

    def relay(s, copies, low, size):
        for side in (0, 1):
            copies[side].wait_recv()
            passed[s].append(pass_on(s, side, low, size))

    def distance(d, g):
        parity = lax.rem(d, 2)
        at = {
            "y": mod4(d // 2 - me["y"]),
            "z": mod4(g // SIDE - me["z"]),
            "x": mod4(lax.rem(g, SIDE) - me["x"]),
        }
        return parity, lax.rem(parity + core, 2), at

    def gathered(s, c, at):
        _, axis_b, axis_c = SPLITS[s]
        b_at, c_at = (at[k] + (at[k] // 2) * (5 - 2 * at[k]) for k in (axis_b, axis_c))
        return ((c * SIDE + c_at) * SIDE + b_at) * 2

    def find(n, carry):
        for i, ref in enumerate((row, col)):
            _, c, at = distance(region[n], ref[n])
            for w, (s, way) in enumerate(ways):
                along, base = at[SPLITS[s][0]], gathered(s, c, at)
                mine_at[w, 2 * n + i] = jnp.where(
                    along == 0, base, jnp.where(along == 2 + toward[w], base + 1, -1)
                )
        return carry

    def plan(n, carry):
        for w, (s, way) in enumerate(ways):
            for i in range(2):
                _, c, at = distance(infos_s[w, 0, n], infos_s[w, 1 + i, n])
                base = gathered(s, c, at)
                pack_at[w, 2 * n + i] = jnp.where(at[SPLITS[s][0]] == 0, base, base + 1)
        return carry

    swapped = [
        send(bufs[s].at[0, halves[w]], bufs[s].at[1, halves[w]], near(SPLITS[s][0], -toward[w]))
        for w, (s, way) in enumerate(ways)
    ]
    own = [spread(s, 0, 1, (1, -1)) for s in each]
    occ_sent = occ_step(0, (1, -1))
    straight = [group(s, 0, 1) for s in each]
    told = [
        send(info, infos.at[w], near(SPLITS[s][0], toward[w])) for w, (s, way) in enumerate(ways)
    ]
    loads[-1].start()

    other = []
    for s in each:
        arrive(own[s])
        own_far = spread(s, 0, 1, (2,))
        arrive(swapped[2 * s : 2 * s + 2])
        other.append(spread(s, 1, 1, (1, -1, 2)) + own_far)
    crossed = [group(s, 1, 1) for s in each]
    arrive(occ_sent)
    occ_sent = occ_step(0, (2,))
    lax.fori_loop(0, held, find, 0)

    near_groups, far_groups = [], []
    for s in each:
        arrive(other[s][:2])
        near_groups.append(group(s, 2, 4))
    arrive(occ_sent)
    occ_sent = occ_step(1, (1, -1, 2))
    for s in each:
        arrive(other[s][2:])
        far_groups.append(group(s, 6, 2))
        mirrored[s].append(mirror(s, 0, unit))
    for s in each:
        relay(s, (straight[s][0], crossed[s][1]), 0, 2)

    arrive(told)
    info_loads = [
        pltpu.make_async_copy(infos.at[w], infos_s.at[w], info_sem.at[w]) for w in range(2 * count)
    ]
    for load in info_loads:
        load.start()
    for load in info_loads:
        load.wait()
    lax.fori_loop(0, held, plan, 0)
    arrive(occ_sent)
    occ_sent = occ_step(2, (1, -1, 2))

    for s in each:
        relay(s, near_groups[s], 2, 4)
    for s in each:
        relay(s, far_groups[s], 6, 2)
        arrive((straight[s][1], crossed[s][0]))
        mirrored[s].append(mirror(s, unit, 2 * unit))
    for s in each:
        arrive(passed[s])
        mirrored[s].append(mirror(s, 3 * unit, unit))
    arrive(occ_sent)
    occ_side = send(oc.at[0], oc.at[1], sibling)
    fetched = []
    for w, (s, way) in enumerate(ways):
        if way == 0:
            arrive(mirrored[s])
        for i in range(2 * held):
            packs[w][i] = bufs[s][pack_at[w, i], halves[w]]
        fetched.append(send(packs[w], gots[w], near(SPLITS[s][0], toward[w])))

    occ_side.wait_recv()
    loads[-1].wait()

    def occ_of(n, ref):
        parity, c, at = distance(region[n], ref[n])
        x, y, z = at["x"], at["y"], at["z"]
        return oc[c, z + parity * (y - z), y + parity * (x - y), x + parity * (z - x)]

    def weigh(n, carry):
        gram = lax.dot_general(
            occ_of(n, row),
            occ_of(n, col),
            (((0,), (0,)), ((), ())),
            preferred_element_type=jnp.float32,
        )
        wg[n] = (gram * wv[n].astype(jnp.float32)).astype(jnp.bfloat16)
        return carry

    lax.fori_loop(0, held, weigh, 0)
    arrive(fetched)

    acc[...] = jnp.zeros_like(acc)

    def whole(n, i):
        parts = []
        for w, (s, way) in enumerate(ways):
            at = mine_at[w, 2 * n + i]
            mine = bufs[s][jnp.maximum(at, 0), halves[w]]
            parts.append(jnp.where(at >= 0, mine, gots[w][2 * n + i]))
        return jnp.concatenate(parts, axis=0)

    def contract(n, carry):
        turned = lax.dot_general(
            whole(n, 0), wg[n], (((0,), (0,)), ((), ())), preferred_element_type=jnp.float32
        ).astype(jnp.bfloat16)
        term = jnp.dot(turned, whole(n, 1), preferred_element_type=jnp.float32)
        for c in range(2):
            for y in range(SIDE):
                hit = region[n] == 2 * mod4(me["y"] + y) + lax.rem(core + c, 2)
                acc[c, y] += jnp.where(hit, term, 0.0)
        return carry

    for n in range(held):
        contract(n, 0)

    swaps = {y: send(acc.at[1, y], part.at[y], sibling) for y in (2, 1, 3, 0)}
    far = lambda k: -sum(min(v, SIDE - v) for v in (k // 16, (k // 4) % 4, k % 4))
    rows = pieces.shape[1]
    sums = []
    for y in swaps:
        swaps[y].wait_recv()
        red[y] = acc[0, y] + part[y]
        for k in sorted(range(y, 64, 4), key=far):
            if k:
                z, x = mod4(me["z"] + k // 16), mod4(me["x"] + (k // 4) % 4)
                piece = red.at[y, pl.ds(pl.multiple_of((z * SIDE + x) * rows, rows), rows)]
                sums.append(send(piece, pieces.at[k], device(z, x, me["y"] + y, core)))
    mine = pl.ds(pl.multiple_of(grp * rows, rows), rows)
    total = red[0, mine]
    arrive(sums)
    for k in range(1, 64):
        total = total + pieces[k]
    pieces[0] = total
    keep = pltpu.make_async_copy(pieces.at[0], out_ref.at[0, mine], info_sem.at[0])
    keep.start()
    done = [
        send(
            pieces.at[0],
            out_ref.at[0, mine],
            device(me["z"] + k // 4, me["x"] + k % 4, me["y"], core),
        )
        for k in sorted(range(1, 16), key=far)
    ]
    arrive(done)
    keep.wait()
    for copy in sent:
        copy.wait_send()


def shards(orbitals, occupied, panel_index, screening, block_region, block_row, block_col):
    held, points = screening.shape[0], screening.shape[1]
    orbs = orbitals.shape[3]
    width = panel_index.shape[0]
    tiles, count = points // 16, len(SPLITS)
    cuts = [0, tiles * 11 // 32, tiles * 11 // 16, tiles]
    slices = [16 * (cuts[s + 1] - cuts[s]) for s in range(count)]
    halves = []
    for rows in slices:
        halves += [16 * ((rows + 31) // 32), rows - 16 * ((rows + 31) // 32)]
    occ_count = occupied.shape[2]
    hbm = pl.BlockSpec(memory_space=pl.ANY)
    dma = pltpu.SemaphoreType.DMA
    return pl.pallas_call(
        functools.partial(kernel, slices),
        out_shape=jax.ShapeDtypeStruct((1, width, width), jnp.float32),
        in_specs=[hbm] * 7,
        out_specs=pl.BlockSpec(memory_space=pl.ANY),
        scratch_shapes=[
            pltpu.VMEM((2 * HALF, rows, width), jnp.bfloat16) for rows in slices
        ]
        + [pltpu.VMEM((2 * held, rows, width), jnp.bfloat16) for rows in halves] * 2
        + [
            pltpu.VMEM((2, SIDE, SIDE, SIDE, occ_count, points), jnp.bfloat16),
            pltpu.VMEM((points, orbs), jnp.bfloat16),
            pltpu.VMEM((1, width), jnp.int32),
            pltpu.VMEM((held, points, points), jnp.bfloat16),
            pltpu.VMEM((held, points, points), jnp.bfloat16),
            pltpu.VMEM((2, SIDE, width, width), jnp.float32),
            pltpu.VMEM((SIDE, width, width), jnp.float32),
            pltpu.VMEM((SIDE, width, width), jnp.float32),
            pltpu.VMEM((64, width // 16, width), jnp.float32),
            pltpu.VMEM((8, 128), jnp.int32),
            pltpu.VMEM((2 * count, 8, 128), jnp.int32),
            pltpu.SMEM((held,), jnp.int32),
            pltpu.SMEM((held,), jnp.int32),
            pltpu.SMEM((held,), jnp.int32),
            pltpu.SMEM((2 * count, 8, 128), jnp.int32),
            pltpu.SMEM((2 * count, 2 * held), jnp.int32),
            pltpu.SMEM((2 * count, 2 * held), jnp.int32),
            dma((7,)),
            dma((2 * count,)),
            dma((COPIES,)),
            dma((COPIES,)),
        ],
        compiler_params=pltpu.CompilerParams(
            collective_id=0, has_side_effects=True, vmem_limit_bytes=56 * 2**20
        ),
    )(
        orbitals,
        occupied,
        panel_index.reshape(1, width),
        screening,
        block_region.reshape(held),
        block_row,
        block_col,
    )


def solution(mesh):
    in_specs = (
        P("reg", "grp", None, None),
        P("reg", "grp", None, None),
        P(),
        P(("grp", "reg"), None, None),
        P(("grp", "reg"), None),
        P(("grp", "reg")),
        P(("grp", "reg")),
    )
    out_specs = P("reg", None, None)
    return jax.shard_map(shards, mesh=mesh, in_specs=in_specs, out_specs=out_specs, check_vma=False)
```

```python
import functools

import jax
import jax.numpy as jnp
from jax import lax
from jax.experimental import pallas as pl
from jax.experimental.pallas import tpu as pltpu
from jax.sharding import PartitionSpec as P

MESH = pl.DeviceIdType.MESH
SIDE = 4
COPIES = 256
SPLITS = (("x", "y", "z"), ("y", "z", "x"), ("z", "x", "y"))
PLACE = {1: 2, -1: 1, 2: 3}
HALF = SIDE * SIDE * 2


def mod4(v):
    return lax.rem(v + 2 * SIDE, SIDE)


def kernel(
    slices,
    orb_hbm,
    occ_hbm,
    pidx_hbm,
    w_hbm,
    region_hbm,
    row_hbm,
    col_hbm,
    out_ref,
    *scratch,
):
    count = len(SPLITS)
    bufs, packs, gots = scratch[:count], scratch[count : 3 * count], scratch[3 * count : 5 * count]
    (oc, orb, pidx, wv, wg, acc, part, red, pieces, info, infos) = scratch[5 * count : 5 * count + 11]
    (region, row, col, infos_s, mine_at, pack_at) = scratch[5 * count + 11 : 5 * count + 17]
    local_sem, info_sem, send_sem, recv_sem = scratch[5 * count + 17 :]
    held = w_hbm.shape[0]
    grp = lax.axis_index("grp")
    reg = lax.axis_index("reg")
    me = {"z": grp // SIDE, "x": lax.rem(grp, SIDE), "y": reg // 2}
    core = lax.rem(reg, 2)

    def device(z, x, y, c):
        return (mod4(z) * SIDE + mod4(x), mod4(y) * 2 + c)

    def near(axis, step):
        at = {k: me[k] + (step if k == axis else 0) for k in me}
        return device(at["z"], at["x"], at["y"], core)

    sibling = (grp, me["y"] * 2 + 1 - core)
    sent = []

    def send(src, dst, to):
        n = len(sent)
        copy = pltpu.make_async_remote_copy(
            src, dst, send_sem.at[n], recv_sem.at[n], device_id=to, device_id_type=MESH
        )
        copy.start()
        sent.append(copy)
        return copy

    loads = [
        pltpu.make_async_copy(src, dst, local_sem.at[i])
        for i, (src, dst) in enumerate(
            [
                (pidx_hbm, pidx),
                (orb_hbm.at[0, 0], orb),
                (occ_hbm.at[0, 0], oc.at[0, 0, 0, 0]),
                (region_hbm, region),
                (row_hbm, row),
                (col_hbm, col),
                (w_hbm, wv),
            ]
        )
    ]
    for load in loads[:-1]:
        load.start()
    barrier = pltpu.get_barrier_semaphore()
    partners = [near(axis, step) for axis in "xyz" for step in (1, -1)] + [sibling]
    for to in partners:
        pl.semaphore_signal(barrier, inc=1, device_id=to, device_id_type=MESH)

    orbs = orb.shape[1]
    width = pidx.shape[1]
    loads[0].wait()
    chosen = (
        lax.broadcasted_iota(jnp.int32, (orbs, width), 0)
        == jnp.broadcast_to(pidx[...], (orbs, width))
    ).astype(jnp.bfloat16)
    loads[1].wait()
    start = 0
    for s, buf in enumerate(bufs):
        buf[0] = jnp.dot(
            orb[start : start + slices[s], :], chosen, preferred_element_type=jnp.float32
        ).astype(jnp.bfloat16)
        start += slices[s]
    for load in loads[2:-1]:
        load.wait()
    sub = lax.broadcasted_iota(jnp.int32, info.shape, 0)
    lane = lax.broadcasted_iota(jnp.int32, info.shape, 1)
    held_info = jnp.zeros(info.shape, jnp.int32)
    for i, ref in enumerate((region, row, col)):
        for n in range(held):
            held_info = jnp.where((sub == i) & (lane == n), ref[n], held_info)
    info[...] = held_info
    pl.semaphore_wait(barrier, len(partners))

    def occ_to(phase, step):
        even, odd = "xyz"[phase], "zxy"[phase]
        at = {k: me[k] + step * ((1 - core) * (k == even) + core * (k == odd)) for k in me}
        return device(at["z"], at["x"], at["y"], core)

    def occ_step(phase, steps):
        inner = (0,) * (3 - phase)
        return [
            send(oc.at[inner + (0,)], oc.at[inner + ((-step) % SIDE,)], occ_to(phase, step))
            for step in steps
        ]

    each = range(count)
    ways = [(s, way) for s in each for way in (0, 1)]
    toward = [(1 - 2 * lax.rem(me[SPLITS[s][0]], 2)) * (1 - 2 * way) for s, way in ways]
    cuts = [16 * ((rows + 31) // 32) for rows in slices]
    halves = [
        pl.ds(0, cuts[s]) if way == 0 else pl.ds(cuts[s], slices[s] - cuts[s]) for s, way in ways
    ]
    unit = 2 * SIDE

    def spread(s, t, size, steps):
        buf, axis = bufs[s], SPLITS[s][1]
        return [
            send(
                buf.at[pl.ds(t, size)],
                buf.at[pl.ds(2 * PLACE[step] + t, size)],
                near(axis, step),
            )
            for step in steps
        ]

    def group(s, low, size):
        buf, axis = bufs[s], SPLITS[s][2]
        return [
            send(
                buf.at[pl.ds(low, size)],
                buf.at[pl.ds(unit * PLACE[step] + low, size)],
                near(axis, step),
            )
            for step in (1, -1)
        ]

    def pass_on(s, side, low, size):
        buf, axis = bufs[s], SPLITS[s][2]
        step = (1, -1)[side]
        low, size = low + side * size // 2, size // 2
        return send(
            buf.at[pl.ds(unit * PLACE[step] + low, size)],
            buf.at[pl.ds(unit * PLACE[2] + low, size)],
            near(axis, step),
        )

    def mirror(s, low, size):
        buf = bufs[s]
        return send(buf.at[pl.ds(low, size)], buf.at[pl.ds(HALF + low, size)], sibling)

    def arrive(copies):
        for copy in copies:
            copy.wait_recv()

    passed, mirrored = [[] for s in each], [[] for s in each]

    def relay(s, copies, low, size):
        for side in (0, 1):
            copies[side].wait_recv()
            passed[s].append(pass_on(s, side, low, size))

    def distance(d, g):
        parity = lax.rem(d, 2)
        at = {
            "y": mod4(d // 2 - me["y"]),
            "z": mod4(g // SIDE - me["z"]),
            "x": mod4(lax.rem(g, SIDE) - me["x"]),
        }
        return parity, lax.rem(parity + core, 2), at

    def gathered(s, c, at):
        _, axis_b, axis_c = SPLITS[s]
        b_at, c_at = (at[k] + (at[k] // 2) * (5 - 2 * at[k]) for k in (axis_b, axis_c))
        return ((c * SIDE + c_at) * SIDE + b_at) * 2

    def find(n, carry):
        for i, ref in enumerate((row, col)):
            _, c, at = distance(region[n], ref[n])
            for w, (s, way) in enumerate(ways):
                along, base = at[SPLITS[s][0]], gathered(s, c, at)
                mine_at[w, 2 * n + i] = jnp.where(
                    along == 0, base, jnp.where(along == 2 + toward[w], base + 1, -1)
                )
        return carry

    def plan(n, carry):
        for w, (s, way) in enumerate(ways):
            for i in range(2):
                _, c, at = distance(infos_s[w, 0, n], infos_s[w, 1 + i, n])
                base = gathered(s, c, at)
                pack_at[w, 2 * n + i] = jnp.where(at[SPLITS[s][0]] == 0, base, base + 1)
        return carry

    swapped = [
        send(bufs[s].at[0, halves[w]], bufs[s].at[1, halves[w]], near(SPLITS[s][0], -toward[w]))
        for w, (s, way) in enumerate(ways)
    ]
    own = [spread(s, 0, 1, (1, -1)) for s in each]
    occ_sent = occ_step(0, (1, -1))
    straight = [group(s, 0, 1) for s in each]
    told = [
        send(info, infos.at[w], near(SPLITS[s][0], toward[w])) for w, (s, way) in enumerate(ways)
    ]
    loads[-1].start()

    other = []
    for s in each:
        arrive(own[s])
        own_far = spread(s, 0, 1, (2,))
        arrive(swapped[2 * s : 2 * s + 2])
        other.append(spread(s, 1, 1, (1, -1, 2)) + own_far)
    crossed = [group(s, 1, 1) for s in each]
    arrive(occ_sent)
    occ_sent = occ_step(0, (2,))
    lax.fori_loop(0, held, find, 0)

    near_groups, far_groups = [], []
    for s in each:
        arrive(other[s][:2])
        near_groups.append(group(s, 2, 4))
    arrive(occ_sent)
    occ_sent = occ_step(1, (1, -1, 2))
    for s in each:
        arrive(other[s][2:])
        far_groups.append(group(s, 6, 2))
        mirrored[s].append(mirror(s, 0, unit))
    for s in each:
        relay(s, (straight[s][0], crossed[s][1]), 0, 2)

    arrive(told)
    info_loads = [
        pltpu.make_async_copy(infos.at[w], infos_s.at[w], info_sem.at[w]) for w in range(2 * count)
    ]
    for load in info_loads:
        load.start()
    for load in info_loads:
        load.wait()
    lax.fori_loop(0, held, plan, 0)
    arrive(occ_sent)
    occ_sent = occ_step(2, (1, -1, 2))

    for s in each:
        relay(s, near_groups[s], 2, 4)
    for s in each:
        relay(s, far_groups[s], 6, 2)
        arrive((straight[s][1], crossed[s][0]))
        mirrored[s].append(mirror(s, unit, 2 * unit))
    for s in each:
        arrive(passed[s])
        mirrored[s].append(mirror(s, 3 * unit, unit))
    arrive(occ_sent)
    occ_side = send(oc.at[0], oc.at[1], sibling)
    fetched = []
    for w, (s, way) in enumerate(ways):
        if way == 0:
            arrive(mirrored[s])
        for i in range(2 * held):
            packs[w][i] = bufs[s][pack_at[w, i], halves[w]]
        fetched.append(send(packs[w], gots[w], near(SPLITS[s][0], toward[w])))

    occ_side.wait_recv()
    loads[-1].wait()

    def occ_of(n, ref):
        parity, c, at = distance(region[n], ref[n])
        x, y, z = at["x"], at["y"], at["z"]
        return oc[c, z + parity * (y - z), y + parity * (x - y), x + parity * (z - x)]

    def weigh(n, carry):
        gram = lax.dot_general(
            occ_of(n, row),
            occ_of(n, col),
            (((0,), (0,)), ((), ())),
            preferred_element_type=jnp.float32,
        )
        wg[n] = (gram * wv[n].astype(jnp.float32)).astype(jnp.bfloat16)
        return carry

    lax.fori_loop(0, held, weigh, 0)
    arrive(fetched)

    acc[...] = jnp.zeros_like(acc)

    def whole(n, i):
        parts = []
        for w, (s, way) in enumerate(ways):
            at = mine_at[w, 2 * n + i]
            mine = bufs[s][jnp.maximum(at, 0), halves[w]]
            parts.append(jnp.where(at >= 0, mine, gots[w][2 * n + i]))
        return jnp.concatenate(parts, axis=0)

    turned = [
        lax.dot_general(
            whole(n, 0), wg[n], (((0,), (0,)), ((), ())), preferred_element_type=jnp.float32
        ).astype(jnp.bfloat16)
        for n in range(held)
    ]
    for n in range(held):
        term = jnp.dot(turned[n], whole(n, 1), preferred_element_type=jnp.float32)
        for c in range(2):
            for y in range(SIDE):
                hit = region[n] == 2 * mod4(me["y"] + y) + lax.rem(core + c, 2)
                acc[c, y] += jnp.where(hit, term, 0.0)

    swaps = {y: send(acc.at[1, y], part.at[y], sibling) for y in (2, 1, 3, 0)}
    far = lambda k: -sum(min(v, SIDE - v) for v in (k // 16, (k // 4) % 4, k % 4))
    rows = pieces.shape[1]
    sums = []
    for y in swaps:
        swaps[y].wait_recv()
        red[y] = acc[0, y] + part[y]
        for k in sorted(range(y, 64, 4), key=far):
            if k:
                z, x = mod4(me["z"] + k // 16), mod4(me["x"] + (k // 4) % 4)
                piece = red.at[y, pl.ds(pl.multiple_of((z * SIDE + x) * rows, rows), rows)]
                sums.append(send(piece, pieces.at[k], device(z, x, me["y"] + y, core)))
    mine = pl.ds(pl.multiple_of(grp * rows, rows), rows)
    total = red[0, mine]
    arrive(sums)
    for k in range(1, 64):
        total = total + pieces[k]
    pieces[0] = total
    keep = pltpu.make_async_copy(pieces.at[0], out_ref.at[0, mine], info_sem.at[0])
    keep.start()
    done = [
        send(
            pieces.at[0],
            out_ref.at[0, mine],
            device(me["z"] + k // 4, me["x"] + k % 4, me["y"], core),
        )
        for k in sorted(range(1, 16), key=far)
    ]
    arrive(done)
    keep.wait()
    for copy in sent:
        copy.wait_send()


def shards(orbitals, occupied, panel_index, screening, block_region, block_row, block_col):
    held, points = screening.shape[0], screening.shape[1]
    orbs = orbitals.shape[3]
    width = panel_index.shape[0]
    tiles, count = points // 16, len(SPLITS)
    cuts = [0, tiles * 11 // 32, tiles * 11 // 16, tiles]
    slices = [16 * (cuts[s + 1] - cuts[s]) for s in range(count)]
    halves = []
    for rows in slices:
        halves += [16 * ((rows + 31) // 32), rows - 16 * ((rows + 31) // 32)]
    occ_count = occupied.shape[2]
    hbm = pl.BlockSpec(memory_space=pl.ANY)
    dma = pltpu.SemaphoreType.DMA
    return pl.pallas_call(
        functools.partial(kernel, slices),
        out_shape=jax.ShapeDtypeStruct((1, width, width), jnp.float32),
        in_specs=[hbm] * 7,
        out_specs=pl.BlockSpec(memory_space=pl.ANY),
        scratch_shapes=[
            pltpu.VMEM((2 * HALF, rows, width), jnp.bfloat16) for rows in slices
        ]
        + [pltpu.VMEM((2 * held, rows, width), jnp.bfloat16) for rows in halves] * 2
        + [
            pltpu.VMEM((2, SIDE, SIDE, SIDE, occ_count, points), jnp.bfloat16),
            pltpu.VMEM((points, orbs), jnp.bfloat16),
            pltpu.VMEM((1, width), jnp.int32),
            pltpu.VMEM((held, points, points), jnp.bfloat16),
            pltpu.VMEM((held, points, points), jnp.bfloat16),
            pltpu.VMEM((2, SIDE, width, width), jnp.float32),
            pltpu.VMEM((SIDE, width, width), jnp.float32),
            pltpu.VMEM((SIDE, width, width), jnp.float32),
            pltpu.VMEM((64, width // 16, width), jnp.float32),
            pltpu.VMEM((8, 128), jnp.int32),
            pltpu.VMEM((2 * count, 8, 128), jnp.int32),
            pltpu.SMEM((held,), jnp.int32),
            pltpu.SMEM((held,), jnp.int32),
            pltpu.SMEM((held,), jnp.int32),
            pltpu.SMEM((2 * count, 8, 128), jnp.int32),
            pltpu.SMEM((2 * count, 2 * held), jnp.int32),
            pltpu.SMEM((2 * count, 2 * held), jnp.int32),
            dma((7,)),
            dma((2 * count,)),
            dma((COPIES,)),
            dma((COPIES,)),
        ],
        compiler_params=pltpu.CompilerParams(
            collective_id=0, has_side_effects=True, vmem_limit_bytes=56 * 2**20
        ),
    )(
        orbitals,
        occupied,
        panel_index.reshape(1, width),
        screening,
        block_region.reshape(held),
        block_row,
        block_col,
    )


def solution(mesh):
    in_specs = (
        P("reg", "grp", None, None),
        P("reg", "grp", None, None),
        P(),
        P(("grp", "reg"), None, None),
        P(("grp", "reg"), None),
        P(("grp", "reg")),
        P(("grp", "reg")),
    )
    out_specs = P("reg", None, None)
    return jax.shard_map(shards, mesh=mesh, in_specs=in_specs, out_specs=out_specs, check_vma=False)
```

```python
import functools

import jax
import jax.numpy as jnp
from jax import lax
from jax.experimental import pallas as pl
from jax.experimental.pallas import tpu as pltpu
from jax.sharding import PartitionSpec as P

MESH = pl.DeviceIdType.MESH
SIDE = 4
COPIES = 256
SPLITS = (("x", "y", "z"), ("y", "z", "x"), ("z", "x", "y"))
PLACE = {1: 2, -1: 1, 2: 3}
HALF = SIDE * SIDE * 2


def mod4(v):
    return lax.rem(v + 2 * SIDE, SIDE)


def kernel(
    slices,
    orb_hbm,
    occ_hbm,
    pidx_hbm,
    w_hbm,
    region_hbm,
    row_hbm,
    col_hbm,
    out_ref,
    *scratch,
):
    count = len(SPLITS)
    bufs, packs, gots = scratch[:count], scratch[count : 3 * count], scratch[3 * count : 5 * count]
    (oc, orb, pidx, wv, wg, acc, part, red, pieces, info, infos) = scratch[5 * count : 5 * count + 11]
    (region, row, col, infos_s, mine_at, pack_at) = scratch[5 * count + 11 : 5 * count + 17]
    local_sem, info_sem, send_sem, recv_sem = scratch[5 * count + 17 :]
    held = w_hbm.shape[0]
    grp = lax.axis_index("grp")
    reg = lax.axis_index("reg")
    me = {"z": grp // SIDE, "x": lax.rem(grp, SIDE), "y": reg // 2}
    core = lax.rem(reg, 2)

    def device(z, x, y, c):
        return (mod4(z) * SIDE + mod4(x), mod4(y) * 2 + c)

    def near(axis, step):
        at = {k: me[k] + (step if k == axis else 0) for k in me}
        return device(at["z"], at["x"], at["y"], core)

    sibling = (grp, me["y"] * 2 + 1 - core)
    sent = []

    def send(src, dst, to):
        n = len(sent)
        copy = pltpu.make_async_remote_copy(
            src, dst, send_sem.at[n], recv_sem.at[n], device_id=to, device_id_type=MESH
        )
        copy.start()
        sent.append(copy)
        return copy

    loads = [
        pltpu.make_async_copy(src, dst, local_sem.at[i])
        for i, (src, dst) in enumerate(
            [
                (pidx_hbm, pidx),
                (orb_hbm.at[0, 0], orb),
                (occ_hbm.at[0, 0], oc.at[0, 0, 0, 0]),
                (region_hbm, region),
                (row_hbm, row),
                (col_hbm, col),
                (w_hbm, wv),
            ]
        )
    ]
    for load in loads[:-1]:
        load.start()
    barrier = pltpu.get_barrier_semaphore()
    partners = [near(axis, step) for axis in "xyz" for step in (1, -1)] + [sibling]
    for to in partners:
        pl.semaphore_signal(barrier, inc=1, device_id=to, device_id_type=MESH)

    orbs = orb.shape[1]
    width = pidx.shape[1]
    loads[0].wait()
    chosen = (
        lax.broadcasted_iota(jnp.int32, (orbs, width), 0)
        == jnp.broadcast_to(pidx[...], (orbs, width))
    ).astype(jnp.bfloat16)
    loads[1].wait()
    start = 0
    for s, buf in enumerate(bufs):
        buf[0] = jnp.dot(
            orb[start : start + slices[s], :], chosen, preferred_element_type=jnp.float32
        ).astype(jnp.bfloat16)
        start += slices[s]
    for load in loads[2:-1]:
        load.wait()
    sub = lax.broadcasted_iota(jnp.int32, info.shape, 0)
    lane = lax.broadcasted_iota(jnp.int32, info.shape, 1)
    held_info = jnp.zeros(info.shape, jnp.int32)
    for i, ref in enumerate((region, row, col)):
        for n in range(held):
            held_info = jnp.where((sub == i) & (lane == n), ref[n], held_info)
    info[...] = held_info
    pl.semaphore_wait(barrier, len(partners))

    def occ_to(phase, step):
        even, odd = "xyz"[phase], "zxy"[phase]
        at = {k: me[k] + step * ((1 - core) * (k == even) + core * (k == odd)) for k in me}
        return device(at["z"], at["x"], at["y"], core)

    def occ_step(phase, steps):
        inner = (0,) * (3 - phase)
        return [
            send(oc.at[inner + (0,)], oc.at[inner + ((-step) % SIDE,)], occ_to(phase, step))
            for step in steps
        ]

    each = range(count)
    ways = [(s, way) for s in each for way in (0, 1)]
    toward = [(1 - 2 * lax.rem(me[SPLITS[s][0]], 2)) * (1 - 2 * way) for s, way in ways]
    cuts = [16 * ((rows + 31) // 32) for rows in slices]
    halves = [
        pl.ds(0, cuts[s]) if way == 0 else pl.ds(cuts[s], slices[s] - cuts[s]) for s, way in ways
    ]
    unit = 2 * SIDE

    def spread(s, t, size, steps):
        buf, axis = bufs[s], SPLITS[s][1]
        return [
            send(
                buf.at[pl.ds(t, size)],
                buf.at[pl.ds(2 * PLACE[step] + t, size)],
                near(axis, step),
            )
            for step in steps
        ]

    def group(s, low, size):
        buf, axis = bufs[s], SPLITS[s][2]
        return [
            send(
                buf.at[pl.ds(low, size)],
                buf.at[pl.ds(unit * PLACE[step] + low, size)],
                near(axis, step),
            )
            for step in (1, -1)
        ]

    def pass_on(s, side, low, size):
        buf, axis = bufs[s], SPLITS[s][2]
        step = (1, -1)[side]
        low, size = low + side * size // 2, size // 2
        return send(
            buf.at[pl.ds(unit * PLACE[step] + low, size)],
            buf.at[pl.ds(unit * PLACE[2] + low, size)],
            near(axis, step),
        )

    def mirror(s, low, size):
        buf = bufs[s]
        return send(buf.at[pl.ds(low, size)], buf.at[pl.ds(HALF + low, size)], sibling)

    def arrive(copies):
        for copy in copies:
            copy.wait_recv()

    passed, mirrored = [[] for s in each], [[] for s in each]

    def relay(s, copies, low, size):
        for side in (0, 1):
            copies[side].wait_recv()
            passed[s].append(pass_on(s, side, low, size))

    def distance(d, g):
        parity = lax.rem(d, 2)
        at = {
            "y": mod4(d // 2 - me["y"]),
            "z": mod4(g // SIDE - me["z"]),
            "x": mod4(lax.rem(g, SIDE) - me["x"]),
        }
        return parity, lax.rem(parity + core, 2), at

    def gathered(s, c, at):
        _, axis_b, axis_c = SPLITS[s]
        b_at, c_at = (at[k] + (at[k] // 2) * (5 - 2 * at[k]) for k in (axis_b, axis_c))
        return ((c * SIDE + c_at) * SIDE + b_at) * 2

    def find(n, carry):
        for i, ref in enumerate((row, col)):
            _, c, at = distance(region[n], ref[n])
            for w, (s, way) in enumerate(ways):
                along, base = at[SPLITS[s][0]], gathered(s, c, at)
                mine_at[w, 2 * n + i] = jnp.where(
                    along == 0, base, jnp.where(along == 2 + toward[w], base + 1, -1)
                )
        return carry

    def plan(n, carry):
        for w, (s, way) in enumerate(ways):
            for i in range(2):
                _, c, at = distance(infos_s[w, 0, n], infos_s[w, 1 + i, n])
                base = gathered(s, c, at)
                pack_at[w, 2 * n + i] = jnp.where(at[SPLITS[s][0]] == 0, base, base + 1)
        return carry

    own = [spread(s, 0, 1, (1, -1)) for s in each]
    swapped = [
        send(bufs[s].at[0, halves[w]], bufs[s].at[1, halves[w]], near(SPLITS[s][0], -toward[w]))
        for w, (s, way) in enumerate(ways)
    ]
    occ_sent = occ_step(0, (1, -1))
    straight = [group(s, 0, 1) for s in each]
    loads[-1].start()

    other = []
    for s in each:
        arrive(own[s])
        own_far = spread(s, 0, 1, (2,))
        arrive(swapped[2 * s : 2 * s + 2])
        other.append(spread(s, 1, 1, (1, -1, 2)) + own_far)
    crossed = [group(s, 1, 1) for s in each]
    arrive(occ_sent)
    occ_sent = occ_step(0, (2,))
    told = [
        send(info, infos.at[w], near(SPLITS[s][0], toward[w])) for w, (s, way) in enumerate(ways)
    ]
    lax.fori_loop(0, held, find, 0)

    near_groups, far_groups = [], []
    for s in each:
        arrive(other[s][:2])
        near_groups.append(group(s, 2, 4))
    arrive(occ_sent)
    occ_sent = occ_step(1, (1, -1, 2))
    for s in each:
        arrive(other[s][2:])
        far_groups.append(group(s, 6, 2))
        mirrored[s].append(mirror(s, 0, unit))
    for s in each:
        relay(s, (straight[s][0], crossed[s][1]), 0, 2)

    arrive(told)
    info_loads = [
        pltpu.make_async_copy(infos.at[w], infos_s.at[w], info_sem.at[w]) for w in range(2 * count)
    ]
    for load in info_loads:
        load.start()
    for load in info_loads:
        load.wait()
    lax.fori_loop(0, held, plan, 0)
    arrive(occ_sent)
    occ_sent = occ_step(2, (1, -1, 2))

    for s in each:
        relay(s, near_groups[s], 2, 4)
    for s in each:
        relay(s, far_groups[s], 6, 2)
        arrive((straight[s][1], crossed[s][0]))
        mirrored[s].append(mirror(s, unit, 2 * unit))
    for s in each:
        arrive(passed[s][:4])
        mirrored[s].append(mirror(s, 3 * unit, 6))
    for s in each:
        arrive(passed[s][4:])
        mirrored[s].append(mirror(s, 3 * unit + 6, 2))
    arrive(occ_sent)
    occ_side = send(oc.at[0], oc.at[1], sibling)
    fetched = []
    for w, (s, way) in enumerate(ways):
        if way == 0:
            arrive(mirrored[s])
        for i in range(2 * held):
            packs[w][i] = bufs[s][pack_at[w, i], halves[w]]
        fetched.append(send(packs[w], gots[w], near(SPLITS[s][0], toward[w])))

    occ_side.wait_recv()
    loads[-1].wait()

    def occ_of(n, ref):
        parity, c, at = distance(region[n], ref[n])
        x, y, z = at["x"], at["y"], at["z"]
        return oc[c, z + parity * (y - z), y + parity * (x - y), x + parity * (z - x)]

    def weigh(n, carry):
        gram = lax.dot_general(
            occ_of(n, row),
            occ_of(n, col),
            (((0,), (0,)), ((), ())),
            preferred_element_type=jnp.float32,
        )
        wg[n] = (gram * wv[n].astype(jnp.float32)).astype(jnp.bfloat16)
        return carry

    lax.fori_loop(0, held, weigh, 0)
    arrive(fetched)

    acc[...] = jnp.zeros_like(acc)

    def whole(n, i):
        parts = []
        for w, (s, way) in enumerate(ways):
            at = mine_at[w, 2 * n + i]
            mine = bufs[s][jnp.maximum(at, 0), halves[w]]
            parts.append(jnp.where(at >= 0, mine, gots[w][2 * n + i]))
        return jnp.concatenate(parts, axis=0)

    turned = [
        lax.dot_general(
            whole(n, 0), wg[n], (((0,), (0,)), ((), ())), preferred_element_type=jnp.float32
        ).astype(jnp.bfloat16)
        for n in range(held)
    ]
    for n in range(held):
        term = jnp.dot(turned[n], whole(n, 1), preferred_element_type=jnp.float32)
        for c in range(2):
            for y in range(SIDE):
                hit = region[n] == 2 * mod4(me["y"] + y) + lax.rem(core + c, 2)
                acc[c, y] += jnp.where(hit, term, 0.0)

    swaps = {y: send(acc.at[1, y], part.at[y], sibling) for y in (2, 1, 3, 0)}
    far = lambda k: -sum(min(v, SIDE - v) for v in (k // 16, (k // 4) % 4, k % 4))
    rows = pieces.shape[1]
    sums = []
    for y in swaps:
        swaps[y].wait_recv()
        red[y] = acc[0, y] + part[y]
        for k in sorted(range(y, 64, 4), key=far):
            if k:
                z, x = mod4(me["z"] + k // 16), mod4(me["x"] + (k // 4) % 4)
                piece = red.at[y, pl.ds(pl.multiple_of((z * SIDE + x) * rows, rows), rows)]
                sums.append(send(piece, pieces.at[k], device(z, x, me["y"] + y, core)))
    mine = pl.ds(pl.multiple_of(grp * rows, rows), rows)
    total = red[0, mine]
    arrive(sums)
    for k in range(1, 64):
        total = total + pieces[k]
    pieces[0] = total
    keep = pltpu.make_async_copy(pieces.at[0], out_ref.at[0, mine], info_sem.at[0])
    keep.start()
    done = [
        send(
            pieces.at[0],
            out_ref.at[0, mine],
            device(me["z"] + k // 4, me["x"] + k % 4, me["y"], core),
        )
        for k in sorted(range(1, 16), key=far)
    ]
    arrive(done)
    keep.wait()
    for copy in sent:
        copy.wait_send()


def shards(orbitals, occupied, panel_index, screening, block_region, block_row, block_col):
    held, points = screening.shape[0], screening.shape[1]
    orbs = orbitals.shape[3]
    width = panel_index.shape[0]
    tiles, count = points // 16, len(SPLITS)
    cuts = [0, tiles * 11 // 32, tiles * 11 // 16, tiles]
    slices = [16 * (cuts[s + 1] - cuts[s]) for s in range(count)]
    halves = []
    for rows in slices:
        halves += [16 * ((rows + 31) // 32), rows - 16 * ((rows + 31) // 32)]
    occ_count = occupied.shape[2]
    hbm = pl.BlockSpec(memory_space=pl.ANY)
    dma = pltpu.SemaphoreType.DMA
    return pl.pallas_call(
        functools.partial(kernel, slices),
        out_shape=jax.ShapeDtypeStruct((1, width, width), jnp.float32),
        in_specs=[hbm] * 7,
        out_specs=pl.BlockSpec(memory_space=pl.ANY),
        scratch_shapes=[
            pltpu.VMEM((2 * HALF, rows, width), jnp.bfloat16) for rows in slices
        ]
        + [pltpu.VMEM((2 * held, rows, width), jnp.bfloat16) for rows in halves] * 2
        + [
            pltpu.VMEM((2, SIDE, SIDE, SIDE, occ_count, points), jnp.bfloat16),
            pltpu.VMEM((points, orbs), jnp.bfloat16),
            pltpu.VMEM((1, width), jnp.int32),
            pltpu.VMEM((held, points, points), jnp.bfloat16),
            pltpu.VMEM((held, points, points), jnp.bfloat16),
            pltpu.VMEM((2, SIDE, width, width), jnp.float32),
            pltpu.VMEM((SIDE, width, width), jnp.float32),
            pltpu.VMEM((SIDE, width, width), jnp.float32),
            pltpu.VMEM((64, width // 16, width), jnp.float32),
            pltpu.VMEM((8, 128), jnp.int32),
            pltpu.VMEM((2 * count, 8, 128), jnp.int32),
            pltpu.SMEM((held,), jnp.int32),
            pltpu.SMEM((held,), jnp.int32),
            pltpu.SMEM((held,), jnp.int32),
            pltpu.SMEM((2 * count, 8, 128), jnp.int32),
            pltpu.SMEM((2 * count, 2 * held), jnp.int32),
            pltpu.SMEM((2 * count, 2 * held), jnp.int32),
            dma((7,)),
            dma((2 * count,)),
            dma((COPIES,)),
            dma((COPIES,)),
        ],
        compiler_params=pltpu.CompilerParams(
            collective_id=0, has_side_effects=True, vmem_limit_bytes=56 * 2**20
        ),
    )(
        orbitals,
        occupied,
        panel_index.reshape(1, width),
        screening,
        block_region.reshape(held),
        block_row,
        block_col,
    )


def solution(mesh):
    in_specs = (
        P("reg", "grp", None, None),
        P("reg", "grp", None, None),
        P(),
        P(("grp", "reg"), None, None),
        P(("grp", "reg"), None),
        P(("grp", "reg")),
        P(("grp", "reg")),
    )
    out_specs = P("reg", None, None)
    return jax.shard_map(shards, mesh=mesh, in_specs=in_specs, out_specs=out_specs, check_vma=False)
```

```python
import functools

import jax
import jax.numpy as jnp
from jax import lax
from jax.experimental import pallas as pl
from jax.experimental.pallas import tpu as pltpu
from jax.sharding import PartitionSpec as P

MESH = pl.DeviceIdType.MESH
SIDE = 4
COPIES = 256
SPLITS = (("x", "y", "z"), ("y", "z", "x"), ("z", "x", "y"))
PLACE = {1: 2, -1: 1, 2: 3}
HALF = SIDE * SIDE * 2


def mod4(v):
    return lax.rem(v + 2 * SIDE, SIDE)


def kernel(
    slices,
    orb_hbm,
    occ_hbm,
    pidx_hbm,
    w_hbm,
    region_hbm,
    row_hbm,
    col_hbm,
    out_ref,
    *scratch,
):
    count = len(SPLITS)
    bufs, packs, gots = scratch[:count], scratch[count : 3 * count], scratch[3 * count : 5 * count]
    (oc, orb, pidx, wv, wg, acc, part, red, pieces, info, infos) = scratch[5 * count : 5 * count + 11]
    (region, row, col, infos_s, mine_at, pack_at) = scratch[5 * count + 11 : 5 * count + 17]
    local_sem, info_sem, send_sem, recv_sem = scratch[5 * count + 17 :]
    held = w_hbm.shape[0]
    grp = lax.axis_index("grp")
    reg = lax.axis_index("reg")
    me = {"z": grp // SIDE, "x": lax.rem(grp, SIDE), "y": reg // 2}
    core = lax.rem(reg, 2)

    def device(z, x, y, c):
        return (mod4(z) * SIDE + mod4(x), mod4(y) * 2 + c)

    def near(axis, step):
        at = {k: me[k] + (step if k == axis else 0) for k in me}
        return device(at["z"], at["x"], at["y"], core)

    sibling = (grp, me["y"] * 2 + 1 - core)
    sent = []

    def send(src, dst, to):
        n = len(sent)
        copy = pltpu.make_async_remote_copy(
            src, dst, send_sem.at[n], recv_sem.at[n], device_id=to, device_id_type=MESH
        )
        copy.start()
        sent.append(copy)
        return copy

    loads = [
        pltpu.make_async_copy(src, dst, local_sem.at[i])
        for i, (src, dst) in enumerate(
            [
                (pidx_hbm, pidx),
                (orb_hbm.at[0, 0], orb),
                (occ_hbm.at[0, 0], oc.at[0, 0, 0, 0]),
                (region_hbm, region),
                (row_hbm, row),
                (col_hbm, col),
                (w_hbm, wv),
            ]
        )
    ]
    for load in loads[:-1]:
        load.start()
    barrier = pltpu.get_barrier_semaphore()
    partners = [near(axis, step) for axis in "xyz" for step in (1, -1)] + [sibling]
    for to in partners:
        pl.semaphore_signal(barrier, inc=1, device_id=to, device_id_type=MESH)

    orbs = orb.shape[1]
    width = pidx.shape[1]
    loads[0].wait()
    chosen = (
        lax.broadcasted_iota(jnp.int32, (orbs, width), 0)
        == jnp.broadcast_to(pidx[...], (orbs, width))
    ).astype(jnp.bfloat16)
    loads[1].wait()
    start = 0
    for s, buf in enumerate(bufs):
        buf[0] = jnp.dot(
            orb[start : start + slices[s], :], chosen, preferred_element_type=jnp.float32
        ).astype(jnp.bfloat16)
        start += slices[s]
    for load in loads[2:-1]:
        load.wait()
    sub = lax.broadcasted_iota(jnp.int32, info.shape, 0)
    lane = lax.broadcasted_iota(jnp.int32, info.shape, 1)
    held_info = jnp.zeros(info.shape, jnp.int32)
    for i, ref in enumerate((region, row, col)):
        for n in range(held):
            held_info = jnp.where((sub == i) & (lane == n), ref[n], held_info)
    info[...] = held_info
    pl.semaphore_wait(barrier, len(partners))

    def occ_to(phase, step):
        even, odd = "xyz"[phase], "zxy"[phase]
        at = {k: me[k] + step * ((1 - core) * (k == even) + core * (k == odd)) for k in me}
        return device(at["z"], at["x"], at["y"], core)

    def occ_step(phase, steps):
        inner = (0,) * (3 - phase)
        return [
            send(oc.at[inner + (0,)], oc.at[inner + ((-step) % SIDE,)], occ_to(phase, step))
            for step in steps
        ]

    each = range(count)
    ways = [(s, way) for s in each for way in (0, 1)]
    toward = [(1 - 2 * lax.rem(me[SPLITS[s][0]], 2)) * (1 - 2 * way) for s, way in ways]
    cuts = [16 * ((rows + 31) // 32) for rows in slices]
    halves = [
        pl.ds(0, cuts[s]) if way == 0 else pl.ds(cuts[s], slices[s] - cuts[s]) for s, way in ways
    ]
    unit = 2 * SIDE

    def spread(s, t, size, steps):
        buf, axis = bufs[s], SPLITS[s][1]
        return [
            send(
                buf.at[pl.ds(t, size)],
                buf.at[pl.ds(2 * PLACE[step] + t, size)],
                near(axis, step),
            )
            for step in steps
        ]

    def group(s, low, size):
        buf, axis = bufs[s], SPLITS[s][2]
        return [
            send(
                buf.at[pl.ds(low, size)],
                buf.at[pl.ds(unit * PLACE[step] + low, size)],
                near(axis, step),
            )
            for step in (1, -1)
        ]

    def pass_on(s, side, low, size):
        buf, axis = bufs[s], SPLITS[s][2]
        step = (1, -1)[side]
        low, size = low + side * size // 2, size // 2
        return send(
            buf.at[pl.ds(unit * PLACE[step] + low, size)],
            buf.at[pl.ds(unit * PLACE[2] + low, size)],
            near(axis, step),
        )

    def mirror(s, low, size):
        buf = bufs[s]
        return send(buf.at[pl.ds(low, size)], buf.at[pl.ds(HALF + low, size)], sibling)

    def arrive(copies):
        for copy in copies:
            copy.wait_recv()

    passed, mirrored = [[] for s in each], [[] for s in each]

    def relay(s, copies, low, size):
        for side in (0, 1):
            copies[side].wait_recv()
            passed[s].append(pass_on(s, side, low, size))

    def distance(d, g):
        parity = lax.rem(d, 2)
        at = {
            "y": mod4(d // 2 - me["y"]),
            "z": mod4(g // SIDE - me["z"]),
            "x": mod4(lax.rem(g, SIDE) - me["x"]),
        }
        return parity, lax.rem(parity + core, 2), at

    def gathered(s, c, at):
        _, axis_b, axis_c = SPLITS[s]
        b_at, c_at = (at[k] + (at[k] // 2) * (5 - 2 * at[k]) for k in (axis_b, axis_c))
        return ((c * SIDE + c_at) * SIDE + b_at) * 2

    def find(n, carry):
        for i, ref in enumerate((row, col)):
            _, c, at = distance(region[n], ref[n])
            for w, (s, way) in enumerate(ways):
                along, base = at[SPLITS[s][0]], gathered(s, c, at)
                mine_at[w, held * i + n] = jnp.where(
                    along == 0, base, jnp.where(along == 2 + toward[w], base + 1, -1)
                )
        return carry

    def plan(n, carry):
        for w, (s, way) in enumerate(ways):
            for i in range(2):
                _, c, at = distance(infos_s[w, 0, n], infos_s[w, 1 + i, n])
                base = gathered(s, c, at)
                pack_at[w, held * i + n] = jnp.where(at[SPLITS[s][0]] == 0, base, base + 1)
        return carry

    own = [spread(s, 0, 1, (1, -1)) for s in each]
    swapped = [
        send(bufs[s].at[0, halves[w]], bufs[s].at[1, halves[w]], near(SPLITS[s][0], -toward[w]))
        for w, (s, way) in enumerate(ways)
    ]
    occ_sent = occ_step(0, (1, -1))
    straight = [group(s, 0, 1) for s in each]
    loads[-1].start()

    other = []
    for s in each:
        arrive(own[s])
        own_far = spread(s, 0, 1, (2,))
        arrive(swapped[2 * s : 2 * s + 2])
        other.append(spread(s, 1, 1, (1, -1, 2)) + own_far)
    crossed = [group(s, 1, 1) for s in each]
    arrive(occ_sent)
    occ_sent = occ_step(0, (2,))
    told = [
        send(info, infos.at[w], near(SPLITS[s][0], toward[w])) for w, (s, way) in enumerate(ways)
    ]
    lax.fori_loop(0, held, find, 0)

    near_groups, far_groups = [], []
    for s in each:
        arrive(other[s][:2])
        near_groups.append(group(s, 2, 4))
    arrive(occ_sent)
    occ_sent = occ_step(1, (1, -1, 2))
    for s in each:
        arrive(other[s][2:])
        far_groups.append(group(s, 6, 2))
        mirrored[s].append(mirror(s, 0, unit))
    for s in each:
        relay(s, (straight[s][0], crossed[s][1]), 0, 2)

    arrive(told)
    info_loads = [
        pltpu.make_async_copy(infos.at[w], infos_s.at[w], info_sem.at[w]) for w in range(2 * count)
    ]
    for load in info_loads:
        load.start()
    for load in info_loads:
        load.wait()
    lax.fori_loop(0, held, plan, 0)
    arrive(occ_sent)
    occ_sent = occ_step(2, (1, -1, 2))

    for s in each:
        relay(s, near_groups[s], 2, 4)
    for s in each:
        relay(s, far_groups[s], 6, 2)
        arrive((straight[s][1], crossed[s][0]))
        mirrored[s].append(mirror(s, unit, 2 * unit))
    for s in each:
        arrive(passed[s][:4])
        mirrored[s].append(mirror(s, 3 * unit, 6))
    for s in each:
        arrive(passed[s][4:])
        mirrored[s].append(mirror(s, 3 * unit + 6, 2))
    arrive(occ_sent)
    occ_side = send(oc.at[0], oc.at[1], sibling)
    fetched = [[], []]
    for i in range(2):
        part_of = pl.ds(held * i, held)
        for w, (s, way) in enumerate(ways):
            if i == 0 and way == 0:
                arrive(mirrored[s])
            for n in range(held * i, held * i + held):
                packs[w][n] = bufs[s][pack_at[w, n], halves[w]]
            to = near(SPLITS[s][0], toward[w])
            fetched[i].append(send(packs[w].at[part_of], gots[w].at[part_of], to))

    occ_side.wait_recv()
    loads[-1].wait()

    def occ_of(n, ref):
        parity, c, at = distance(region[n], ref[n])
        x, y, z = at["x"], at["y"], at["z"]
        return oc[c, z + parity * (y - z), y + parity * (x - y), x + parity * (z - x)]

    def weigh(n, carry):
        gram = lax.dot_general(
            occ_of(n, row),
            occ_of(n, col),
            (((0,), (0,)), ((), ())),
            preferred_element_type=jnp.float32,
        )
        wg[n] = (gram * wv[n].astype(jnp.float32)).astype(jnp.bfloat16)
        return carry

    lax.fori_loop(0, held, weigh, 0)
    arrive(fetched[0])

    acc[...] = jnp.zeros_like(acc)

    def whole(n, i):
        parts = []
        for w, (s, way) in enumerate(ways):
            at = mine_at[w, held * i + n]
            mine = bufs[s][jnp.maximum(at, 0), halves[w]]
            parts.append(jnp.where(at >= 0, mine, gots[w][held * i + n]))
        return jnp.concatenate(parts, axis=0)

    turned = [
        lax.dot_general(
            whole(n, 0), wg[n], (((0,), (0,)), ((), ())), preferred_element_type=jnp.float32
        ).astype(jnp.bfloat16)
        for n in range(held)
    ]
    arrive(fetched[1])
    for n in range(held):
        term = jnp.dot(turned[n], whole(n, 1), preferred_element_type=jnp.float32)
        for c in range(2):
            for y in range(SIDE):
                hit = region[n] == 2 * mod4(me["y"] + y) + lax.rem(core + c, 2)
                acc[c, y] += jnp.where(hit, term, 0.0)

    swaps = {y: send(acc.at[1, y], part.at[y], sibling) for y in (2, 1, 3, 0)}
    far = lambda k: -sum(min(v, SIDE - v) for v in (k // 16, (k // 4) % 4, k % 4))
    rows = pieces.shape[1]
    sums = []
    for y in swaps:
        swaps[y].wait_recv()
        red[y] = acc[0, y] + part[y]
        for k in sorted(range(y, 64, 4), key=far):
            if k:
                z, x = mod4(me["z"] + k // 16), mod4(me["x"] + (k // 4) % 4)
                piece = red.at[y, pl.ds(pl.multiple_of((z * SIDE + x) * rows, rows), rows)]
                sums.append(send(piece, pieces.at[k], device(z, x, me["y"] + y, core)))
    mine = pl.ds(pl.multiple_of(grp * rows, rows), rows)
    total = red[0, mine]
    arrive(sums)
    for k in range(1, 64):
        total = total + pieces[k]
    pieces[0] = total
    keep = pltpu.make_async_copy(pieces.at[0], out_ref.at[0, mine], info_sem.at[0])
    keep.start()
    done = [
        send(
            pieces.at[0],
            out_ref.at[0, mine],
            device(me["z"] + k // 4, me["x"] + k % 4, me["y"], core),
        )
        for k in sorted(range(1, 16), key=far)
    ]
    arrive(done)
    keep.wait()
    for copy in sent:
        copy.wait_send()


def shards(orbitals, occupied, panel_index, screening, block_region, block_row, block_col):
    held, points = screening.shape[0], screening.shape[1]
    orbs = orbitals.shape[3]
    width = panel_index.shape[0]
    tiles, count = points // 16, len(SPLITS)
    cuts = [0, tiles * 11 // 32, tiles * 11 // 16, tiles]
    slices = [16 * (cuts[s + 1] - cuts[s]) for s in range(count)]
    halves = []
    for rows in slices:
        halves += [16 * ((rows + 31) // 32), rows - 16 * ((rows + 31) // 32)]
    occ_count = occupied.shape[2]
    hbm = pl.BlockSpec(memory_space=pl.ANY)
    dma = pltpu.SemaphoreType.DMA
    return pl.pallas_call(
        functools.partial(kernel, slices),
        out_shape=jax.ShapeDtypeStruct((1, width, width), jnp.float32),
        in_specs=[hbm] * 7,
        out_specs=pl.BlockSpec(memory_space=pl.ANY),
        scratch_shapes=[
            pltpu.VMEM((2 * HALF, rows, width), jnp.bfloat16) for rows in slices
        ]
        + [pltpu.VMEM((2 * held, rows, width), jnp.bfloat16) for rows in halves] * 2
        + [
            pltpu.VMEM((2, SIDE, SIDE, SIDE, occ_count, points), jnp.bfloat16),
            pltpu.VMEM((points, orbs), jnp.bfloat16),
            pltpu.VMEM((1, width), jnp.int32),
            pltpu.VMEM((held, points, points), jnp.bfloat16),
            pltpu.VMEM((held, points, points), jnp.bfloat16),
            pltpu.VMEM((2, SIDE, width, width), jnp.float32),
            pltpu.VMEM((SIDE, width, width), jnp.float32),
            pltpu.VMEM((SIDE, width, width), jnp.float32),
            pltpu.VMEM((64, width // 16, width), jnp.float32),
            pltpu.VMEM((8, 128), jnp.int32),
            pltpu.VMEM((2 * count, 8, 128), jnp.int32),
            pltpu.SMEM((held,), jnp.int32),
            pltpu.SMEM((held,), jnp.int32),
            pltpu.SMEM((held,), jnp.int32),
            pltpu.SMEM((2 * count, 8, 128), jnp.int32),
            pltpu.SMEM((2 * count, 2 * held), jnp.int32),
            pltpu.SMEM((2 * count, 2 * held), jnp.int32),
            dma((7,)),
            dma((2 * count,)),
            dma((COPIES,)),
            dma((COPIES,)),
        ],
        compiler_params=pltpu.CompilerParams(
            collective_id=0, has_side_effects=True, vmem_limit_bytes=56 * 2**20
        ),
    )(
        orbitals,
        occupied,
        panel_index.reshape(1, width),
        screening,
        block_region.reshape(held),
        block_row,
        block_col,
    )


def solution(mesh):
    in_specs = (
        P("reg", "grp", None, None),
        P("reg", "grp", None, None),
        P(),
        P(("grp", "reg"), None, None),
        P(("grp", "reg"), None),
        P(("grp", "reg")),
        P(("grp", "reg")),
    )
    out_specs = P("reg", None, None)
    return jax.shard_map(shards, mesh=mesh, in_specs=in_specs, out_specs=out_specs, check_vma=False)
```

```python
import functools

import jax
import jax.numpy as jnp
from jax import lax
from jax.experimental import pallas as pl
from jax.experimental.pallas import tpu as pltpu
from jax.sharding import PartitionSpec as P

MESH = pl.DeviceIdType.MESH
SIDE = 4
COPIES = 256
SPLITS = (("x", "y", "z"), ("y", "z", "x"), ("z", "x", "y"))
PLACE = {1: 2, -1: 1, 2: 3}
HALF = SIDE * SIDE * 2


def mod4(v):
    return lax.rem(v + 2 * SIDE, SIDE)


def kernel(
    slices,
    orb_hbm,
    occ_hbm,
    pidx_hbm,
    w_hbm,
    region_hbm,
    row_hbm,
    col_hbm,
    out_ref,
    *scratch,
):
    count = len(SPLITS)
    bufs, packs, gots = scratch[:count], scratch[count : 3 * count], scratch[3 * count : 5 * count]
    (oc, orb, pidx, wv, wg, acc, part, red, pieces, info, infos) = scratch[5 * count : 5 * count + 11]
    (region, row, col, infos_s, mine_at, pack_at) = scratch[5 * count + 11 : 5 * count + 17]
    local_sem, info_sem, send_sem, recv_sem = scratch[5 * count + 17 :]
    held = w_hbm.shape[0]
    grp = lax.axis_index("grp")
    reg = lax.axis_index("reg")
    me = {"z": grp // SIDE, "x": lax.rem(grp, SIDE), "y": reg // 2}
    core = lax.rem(reg, 2)

    def device(z, x, y, c):
        return (mod4(z) * SIDE + mod4(x), mod4(y) * 2 + c)

    def near(axis, step):
        at = {k: me[k] + (step if k == axis else 0) for k in me}
        return device(at["z"], at["x"], at["y"], core)

    sibling = (grp, me["y"] * 2 + 1 - core)
    sent = []

    def send(src, dst, to):
        n = len(sent)
        copy = pltpu.make_async_remote_copy(
            src, dst, send_sem.at[n], recv_sem.at[n], device_id=to, device_id_type=MESH
        )
        copy.start()
        sent.append(copy)
        return copy

    loads = [
        pltpu.make_async_copy(src, dst, local_sem.at[i])
        for i, (src, dst) in enumerate(
            [
                (pidx_hbm, pidx),
                (orb_hbm.at[0, 0], orb),
                (occ_hbm.at[0, 0], oc.at[0, 0, 0, 0]),
                (region_hbm, region),
                (row_hbm, row),
                (col_hbm, col),
                (w_hbm, wv),
            ]
        )
    ]
    for load in loads[:-1]:
        load.start()
    barrier = pltpu.get_barrier_semaphore()
    partners = [near(axis, step) for axis in "xyz" for step in (1, -1)] + [sibling]
    for to in partners:
        pl.semaphore_signal(barrier, inc=1, device_id=to, device_id_type=MESH)

    orbs = orb.shape[1]
    width = pidx.shape[1]
    loads[0].wait()
    chosen = (
        lax.broadcasted_iota(jnp.int32, (orbs, width), 0)
        == jnp.broadcast_to(pidx[...], (orbs, width))
    ).astype(jnp.bfloat16)
    loads[1].wait()
    start = 0
    for s, buf in enumerate(bufs):
        buf[0] = jnp.dot(
            orb[start : start + slices[s], :], chosen, preferred_element_type=jnp.float32
        ).astype(jnp.bfloat16)
        start += slices[s]
    for load in loads[2:-1]:
        load.wait()
    sub = lax.broadcasted_iota(jnp.int32, info.shape, 0)
    lane = lax.broadcasted_iota(jnp.int32, info.shape, 1)
    held_info = jnp.zeros(info.shape, jnp.int32)
    for i, ref in enumerate((region, row, col)):
        for n in range(held):
            held_info = jnp.where((sub == i) & (lane == n), ref[n], held_info)
    info[...] = held_info
    pl.semaphore_wait(barrier, len(partners))

    def occ_to(phase, step):
        even, odd = "xyz"[phase], "zxy"[phase]
        at = {k: me[k] + step * ((1 - core) * (k == even) + core * (k == odd)) for k in me}
        return device(at["z"], at["x"], at["y"], core)

    def occ_step(phase, steps):
        inner = (0,) * (3 - phase)
        return [
            send(oc.at[inner + (0,)], oc.at[inner + ((-step) % SIDE,)], occ_to(phase, step))
            for step in steps
        ]

    each = range(count)
    ways = [(s, way) for s in each for way in (0, 1)]
    toward = [(1 - 2 * lax.rem(me[SPLITS[s][0]], 2)) * (1 - 2 * way) for s, way in ways]
    cuts = [16 * ((rows + 31) // 32) for rows in slices]
    halves = [
        pl.ds(0, cuts[s]) if way == 0 else pl.ds(cuts[s], slices[s] - cuts[s]) for s, way in ways
    ]
    unit = 2 * SIDE

    def spread(s, t, size, steps):
        buf, axis = bufs[s], SPLITS[s][1]
        return [
            send(
                buf.at[pl.ds(t, size)],
                buf.at[pl.ds(2 * PLACE[step] + t, size)],
                near(axis, step),
            )
            for step in steps
        ]

    def group(s, low, size):
        buf, axis = bufs[s], SPLITS[s][2]
        return [
            send(
                buf.at[pl.ds(low, size)],
                buf.at[pl.ds(unit * PLACE[step] + low, size)],
                near(axis, step),
            )
            for step in (1, -1)
        ]

    def pass_on(s, side, low, size):
        buf, axis = bufs[s], SPLITS[s][2]
        step = (1, -1)[side]
        low, size = low + side * size // 2, size // 2
        return send(
            buf.at[pl.ds(unit * PLACE[step] + low, size)],
            buf.at[pl.ds(unit * PLACE[2] + low, size)],
            near(axis, step),
        )

    def mirror(s, low, size):
        buf = bufs[s]
        return send(buf.at[pl.ds(low, size)], buf.at[pl.ds(HALF + low, size)], sibling)

    def arrive(copies):
        for copy in copies:
            copy.wait_recv()

    passed, mirrored = [[] for s in each], [[] for s in each]

    def relay(s, copies, low, size):
        for side in (0, 1):
            copies[side].wait_recv()
            passed[s].append(pass_on(s, side, low, size))

    def distance(d, g):
        parity = lax.rem(d, 2)
        at = {
            "y": mod4(d // 2 - me["y"]),
            "z": mod4(g // SIDE - me["z"]),
            "x": mod4(lax.rem(g, SIDE) - me["x"]),
        }
        return parity, lax.rem(parity + core, 2), at

    def gathered(s, c, at):
        _, axis_b, axis_c = SPLITS[s]
        b_at, c_at = (at[k] + (at[k] // 2) * (5 - 2 * at[k]) for k in (axis_b, axis_c))
        return ((c * SIDE + c_at) * SIDE + b_at) * 2

    def find(n, carry):
        for i, ref in enumerate((row, col)):
            _, c, at = distance(region[n], ref[n])
            for w, (s, way) in enumerate(ways):
                along, base = at[SPLITS[s][0]], gathered(s, c, at)
                mine_at[w, held * i + n] = jnp.where(
                    along == 0, base, jnp.where(along == 2 + toward[w], base + 1, -1)
                )
        return carry

    def plan(n, carry):
        for w, (s, way) in enumerate(ways):
            for i in range(2):
                _, c, at = distance(infos_s[w, 0, n], infos_s[w, 1 + i, n])
                base = gathered(s, c, at)
                pack_at[w, held * i + n] = jnp.where(at[SPLITS[s][0]] == 0, base, base + 1)
        return carry

    own = [spread(s, 0, 1, (1, -1)) for s in each]
    swapped = [
        send(bufs[s].at[0, halves[w]], bufs[s].at[1, halves[w]], near(SPLITS[s][0], -toward[w]))
        for w, (s, way) in enumerate(ways)
    ]
    occ_sent = occ_step(0, (1, -1))
    straight = [group(s, 0, 1) for s in each]
    loads[-1].start()

    other = []
    for s in each:
        arrive(own[s])
        own_far = spread(s, 0, 1, (2,))
        arrive(swapped[2 * s : 2 * s + 2])
        other.append(spread(s, 1, 1, (1, -1, 2)) + own_far)
    crossed = [group(s, 1, 1) for s in each]
    arrive(occ_sent)
    occ_sent = occ_step(0, (2,))
    told = [
        send(info, infos.at[w], near(SPLITS[s][0], toward[w])) for w, (s, way) in enumerate(ways)
    ]
    lax.fori_loop(0, held, find, 0)

    near_groups, far_groups = [], []
    for s in each:
        arrive(other[s][:2])
        near_groups.append(group(s, 2, 4))
    arrive(occ_sent)
    occ_sent = occ_step(1, (1, -1, 2))
    for s in each:
        arrive(other[s][2:])
        far_groups.append(group(s, 6, 2))
        mirrored[s].append(mirror(s, 0, unit))
    for s in each:
        relay(s, (straight[s][0], crossed[s][1]), 0, 2)

    arrive(told)
    info_loads = [
        pltpu.make_async_copy(infos.at[w], infos_s.at[w], info_sem.at[w]) for w in range(2 * count)
    ]
    for load in info_loads:
        load.start()
    for load in info_loads:
        load.wait()
    lax.fori_loop(0, held, plan, 0)
    arrive(occ_sent)
    occ_sent = occ_step(2, (1, -1, 2))

    for s in each:
        relay(s, near_groups[s], 2, 4)
    for s in each:
        relay(s, far_groups[s], 6, 2)
        arrive((straight[s][1], crossed[s][0]))
        mirrored[s].append(mirror(s, unit, 2 * unit))
    for s in each:
        arrive(passed[s][:4])
        mirrored[s].append(mirror(s, 3 * unit, 6))
    for s in each:
        arrive(passed[s][4:])
        mirrored[s].append(mirror(s, 3 * unit + 6, 2))
    arrive(occ_sent)
    occ_side = send(oc.at[0], oc.at[1], sibling)
    fetched = [[], []]
    for i in range(2):
        part_of = pl.ds(held * i, held)
        for w, (s, way) in enumerate(ways):
            if i == 0 and way == 0:
                arrive(mirrored[s])
            for n in range(held * i, held * i + held):
                packs[w][n] = bufs[s][pack_at[w, n], halves[w]]
            to = near(SPLITS[s][0], toward[w])
            fetched[i].append(send(packs[w].at[part_of], gots[w].at[part_of], to))

    occ_side.wait_recv()
    loads[-1].wait()

    def occ_of(n, ref):
        parity, c, at = distance(region[n], ref[n])
        x, y, z = at["x"], at["y"], at["z"]
        return oc[c, z + parity * (y - z), y + parity * (x - y), x + parity * (z - x)]

    def weigh(n, carry):
        gram = lax.dot_general(
            occ_of(n, row),
            occ_of(n, col),
            (((0,), (0,)), ((), ())),
            preferred_element_type=jnp.float32,
        )
        wg[n] = (gram * wv[n].astype(jnp.float32)).astype(jnp.bfloat16)
        return carry

    lax.fori_loop(0, held, weigh, 0)
    acc[...] = jnp.zeros_like(acc)
    arrive(fetched[0])


    def whole(n, i):
        parts = []
        for w, (s, way) in enumerate(ways):
            at = mine_at[w, held * i + n]
            mine = bufs[s][jnp.maximum(at, 0), halves[w]]
            parts.append(jnp.where(at >= 0, mine, gots[w][held * i + n]))
        return jnp.concatenate(parts, axis=0)

    turned = [
        lax.dot_general(
            whole(n, 0), wg[n], (((0,), (0,)), ((), ())), preferred_element_type=jnp.float32
        ).astype(jnp.bfloat16)
        for n in range(held)
    ]
    arrive(fetched[1])
    for n in range(held):
        term = jnp.dot(turned[n], whole(n, 1), preferred_element_type=jnp.float32)
        for c in range(2):
            for y in range(SIDE):
                hit = region[n] == 2 * mod4(me["y"] + y) + lax.rem(core + c, 2)
                acc[c, y] += jnp.where(hit, term, 0.0)

    swaps = {y: send(acc.at[1, y], part.at[y], sibling) for y in (2, 1, 3, 0)}
    far = lambda k: -sum(min(v, SIDE - v) for v in (k // 16, (k // 4) % 4, k % 4))
    rows = pieces.shape[1]
    sums = []
    for y in swaps:
        swaps[y].wait_recv()
        red[y] = acc[0, y] + part[y]
        for k in sorted(range(y, 64, 4), key=far):
            if k:
                z, x = mod4(me["z"] + k // 16), mod4(me["x"] + (k // 4) % 4)
                piece = red.at[y, pl.ds(pl.multiple_of((z * SIDE + x) * rows, rows), rows)]
                sums.append(send(piece, pieces.at[k], device(z, x, me["y"] + y, core)))
    mine = pl.ds(pl.multiple_of(grp * rows, rows), rows)
    total = red[0, mine]
    arrive(sums)
    for k in range(1, 64):
        total = total + pieces[k]
    pieces[0] = total
    keep = pltpu.make_async_copy(pieces.at[0], out_ref.at[0, mine], info_sem.at[0])
    keep.start()
    done = [
        send(
            pieces.at[0],
            out_ref.at[0, mine],
            device(me["z"] + k // 4, me["x"] + k % 4, me["y"], core),
        )
        for k in sorted(range(1, 16), key=far)
    ]
    arrive(done)
    keep.wait()
    for copy in sent:
        copy.wait_send()


def shards(orbitals, occupied, panel_index, screening, block_region, block_row, block_col):
    held, points = screening.shape[0], screening.shape[1]
    orbs = orbitals.shape[3]
    width = panel_index.shape[0]
    tiles, count = points // 16, len(SPLITS)
    cuts = [0, tiles * 11 // 32, tiles * 11 // 16, tiles]
    slices = [16 * (cuts[s + 1] - cuts[s]) for s in range(count)]
    halves = []
    for rows in slices:
        halves += [16 * ((rows + 31) // 32), rows - 16 * ((rows + 31) // 32)]
    occ_count = occupied.shape[2]
    hbm = pl.BlockSpec(memory_space=pl.ANY)
    dma = pltpu.SemaphoreType.DMA
    return pl.pallas_call(
        functools.partial(kernel, slices),
        out_shape=jax.ShapeDtypeStruct((1, width, width), jnp.float32),
        in_specs=[hbm] * 7,
        out_specs=pl.BlockSpec(memory_space=pl.ANY),
        scratch_shapes=[
            pltpu.VMEM((2 * HALF, rows, width), jnp.bfloat16) for rows in slices
        ]
        + [pltpu.VMEM((2 * held, rows, width), jnp.bfloat16) for rows in halves] * 2
        + [
            pltpu.VMEM((2, SIDE, SIDE, SIDE, occ_count, points), jnp.bfloat16),
            pltpu.VMEM((points, orbs), jnp.bfloat16),
            pltpu.VMEM((1, width), jnp.int32),
            pltpu.VMEM((held, points, points), jnp.bfloat16),
            pltpu.VMEM((held, points, points), jnp.bfloat16),
            pltpu.VMEM((2, SIDE, width, width), jnp.float32),
            pltpu.VMEM((SIDE, width, width), jnp.float32),
            pltpu.VMEM((SIDE, width, width), jnp.float32),
            pltpu.VMEM((64, width // 16, width), jnp.float32),
            pltpu.VMEM((8, 128), jnp.int32),
            pltpu.VMEM((2 * count, 8, 128), jnp.int32),
            pltpu.SMEM((held,), jnp.int32),
            pltpu.SMEM((held,), jnp.int32),
            pltpu.SMEM((held,), jnp.int32),
            pltpu.SMEM((2 * count, 8, 128), jnp.int32),
            pltpu.SMEM((2 * count, 2 * held), jnp.int32),
            pltpu.SMEM((2 * count, 2 * held), jnp.int32),
            dma((7,)),
            dma((2 * count,)),
            dma((COPIES,)),
            dma((COPIES,)),
        ],
        compiler_params=pltpu.CompilerParams(
            collective_id=0, has_side_effects=True, vmem_limit_bytes=56 * 2**20
        ),
    )(
        orbitals,
        occupied,
        panel_index.reshape(1, width),
        screening,
        block_region.reshape(held),
        block_row,
        block_col,
    )


def solution(mesh):
    in_specs = (
        P("reg", "grp", None, None),
        P("reg", "grp", None, None),
        P(),
        P(("grp", "reg"), None, None),
        P(("grp", "reg"), None),
        P(("grp", "reg")),
        P(("grp", "reg")),
    )
    out_specs = P("reg", None, None)
    return jax.shard_map(shards, mesh=mesh, in_specs=in_specs, out_specs=out_specs, check_vma=False)
```
